32 devices in a mesh: dp: 4 (over y, core), tensor: 8 (over z, x).
Axes of the slice: x: 2, y: 2, z: 4, core: 2. Of those that a mesh axis runs over, the one named last changes fastest.
Arguments:
- tokens: bfloat16 [3072, 8192], P('dp', 'tensor'), may hold values from -6 to 6
- cotangent: bfloat16 [3072, 512], P('dp', 'tensor'), may hold values from -0.0625 to 0.0625
- frozen_value_weight: bfloat16 [8192, 512], P('tensor'), may hold values from -0.0625 to 0.0625
- adapter_down_weight: bfloat16 [8, 32, 8192], P('tensor'), may hold values from -0.0625 to 0.0625
- adapter_up_weight: bfloat16 [8, 32, 512], P('tensor'), may hold values from -1 to 1
- member: int32 [24, 1], P('dp'), may hold values from 0 to 7; in each aligned block of 6 rows (0 to 5, 6 to 11, ...) at most 2 rows name the same one
Outputs:
- output: bfloat16 [3072, 512], P(('dp', 'tensor'))
- grad_down: float32 [8, 32, 8192], P('tensor', None, 'dp')
- grad_up: float32 [8, 32, 512], P('tensor', 'dp')
The draws below stay inside these ranges and needn't reach their ends.
Inputs may be any that keep to these rules, and one draw needn't show every extreme that they name: Within the 6 blocks of one data index no member appears more than 2 times, and some member appears exactly 2 times there.
All inputs are finite; a program needn't handle non-finite values.
Results may differ from the reference program's by a relative error of at most 0.015.
Values may be sent and summed in bfloat16 or wider, within the bound.
A program may use at most 64 MiB of HBM per device.

```python
import math
import jax
import jax.numpy as jnp
import numpy as np
from jax import lax

MODEL_WIDTH = 8192
VALUE_FEATURES = 512
ADAPTER_RANK = 32
BLK = 128
CAP = 2
MEMBER_COUNT = 8
NB = 6
ROWS = 768
TOKENS = 3072
N_DP = 4
N_TENSOR = 8


def raised(array, key, source, target, blocks, factor):
    def block_of(dim):
        return (jnp.arange(array.shape[dim]) // (array.shape[dim] // blocks)).reshape((-1,) + (1,) * (array.ndim - 1 - dim))

    near = jax.random.permutation(key, blocks)[block_of(target)]
    far = (block_of(target) + blocks // 2) % blocks
    return jnp.where((block_of(source) == near) | (block_of(source) == far), factor * array, array)


def shard_levels(stream_key, dims, pieces, least, high):
    level, own = 1.0, jax.random.fold_in(stream_key, 6)
    for position, blocks in pieces:
        draws = jnp.exp(jax.random.uniform(jax.random.fold_in(own, position), (blocks,), jnp.float32, least / len(pieces), high / len(pieces)))
        level = level * jnp.repeat(draws, dims[position] // blocks).reshape([-1 if axis == position else 1 for axis in range(len(dims))])
    return level


def deal_out(key, own, number, rows, amount, top, most, slope):
    ranking = jax.random.permutation(key, amount)
    packed, usual = load_shares(amount, rows * top, most, slope, True), load_shares(amount, rows * top, most, slope, False)
    places = jnp.arange(amount)

    def named(sizes, rotation):
        used = int((sizes > 0).sum())
        fixed = max(1, used // 4)
        passed = fixed + (places - fixed + rotation * (used - fixed)) % max(1, amount - fixed)
        return jnp.zeros((amount,), jnp.int32).at[ranking[jnp.where(places < fixed, places, passed)]].set(jnp.asarray(sizes, jnp.int32))

    sizes = jnp.where(number % 4 == 0, named(packed, number // 4), named(usual, number - number // 4 - 1))
    mixed = jax.random.permutation(jax.random.fold_in(own, 3), amount)
    source_of, taker = mixed[0:amount // 2 * 2:2], mixed[1:amount // 2 * 2:2]
    room = jnp.minimum(sizes[source_of] - 1, most - sizes[taker]) // 2
    room = jnp.where((source_of == ranking[0]) | (taker == ranking[0]) | (sizes[taker] == 0), 0, jnp.maximum(room, 0))
    passed = jax.random.randint(jax.random.fold_in(own, 4), (amount // 2,), 0, 1 << 20) % (room + 1)
    sizes = sizes.at[source_of].add(-passed).at[taker].add(passed)
    items = jnp.searchsorted(jnp.cumsum(sizes), jnp.arange(rows * top), side="right").astype(jnp.int32)
    grid = items.reshape(top, rows).T
    grid = grid[jax.random.permutation(jax.random.fold_in(own, 1), rows)]
    rotation = jax.random.randint(jax.random.fold_in(own, 2), (rows, 1), 0, top)
    return jnp.take_along_axis(grid, (jnp.arange(top)[None, :] + rotation) % top, axis=1)


def load_shares(count, total, limit, lean, full):
    weights = [(1 << 20) // math.isqrt(rank ** lean) + 1 for rank in range(1, count + 1)]
    largest = limit if full else min(limit, max(-(-total // count), total * weights[0] // sum(weights)))
    least = 1 if total - largest >= count - 1 else 0
    holding, rest = [largest] + [least] * (count - 1), total - largest - least * (count - 1)
    while rest > 0:
        free = [i for i in range(1, count) if holding[i] < largest] or [i for i in range(1, count) if holding[i] < limit]
        whole, budget = sum([weights[i] for i in free]), rest
        for i in free:
            more = min(limit - holding[i], max(1, budget * weights[i] // whole), rest)
            holding[i] = holding[i] + more
            rest = rest - more
    return np.array(holding)


def gaussian(key, extent, spread, most, shards=(), held_as=jnp.bfloat16):
    level = shard_levels(key, extent, shards, -0.22, 0.18) if shards else 1.0
    values = jax.random.normal(key, extent, jnp.float32) * spread * level
    return jnp.minimum(jnp.maximum(values, -most), most).astype(held_as)


def noise_with(key, extent, scale, limit, pieces, heavy, dtype=jnp.bfloat16):
    values = scale * jax.random.normal(key, extent, jnp.float32)
    if pieces:
        values = values * shard_levels(key, extent, pieces, -0.22, 0.18)
    return jnp.clip(raised(values, jax.random.fold_in(key, 3), *heavy), -limit, limit).astype(dtype)


def setup_inputs(seed: int = 0) -> dict:
    keys = jax.random.split(jax.random.key(seed), 7)
    tokens = noise_with(keys[0], (TOKENS, MODEL_WIDTH), 1.0, 6.0, ((0, 4), (1, 8)), (1, 0, 8, 2.0))
    cotangent = gaussian(keys[1], (TOKENS, VALUE_FEATURES), (0.25 / (BLK * N_DP) ** 0.5), 0.0625, ((0, 4), (1, 8)))
    frozen_value_weight = gaussian(keys[2], (MODEL_WIDTH, VALUE_FEATURES), MODEL_WIDTH ** -0.5, 0.0625, ((0, 8),))
    adapter_down_weight = gaussian(keys[3], (MEMBER_COUNT, ADAPTER_RANK, MODEL_WIDTH), MODEL_WIDTH ** -0.5, 0.0625, ((0, 8),))
    adapter_up_weight = gaussian(keys[4], (MEMBER_COUNT, ADAPTER_RANK, VALUE_FEATURES), ADAPTER_RANK ** -0.5, 1.0, ((0, 8),))
    member_keys = jax.random.split(jax.random.fold_in(keys[5], 1), (NB * N_DP) // NB)
    member_turns = jax.random.permutation(jax.random.fold_in(keys[5], 3), (NB * N_DP) // NB)
    member = jax.vmap(lambda own, number: deal_out(jax.random.fold_in(keys[5], 2), own, number, NB, MEMBER_COUNT, 1, CAP, 2))(member_keys, member_turns).reshape((NB * N_DP, 1))
    return dict(tokens=tokens, cotangent=cotangent, frozen_value_weight=frozen_value_weight, adapter_down_weight=adapter_down_weight, adapter_up_weight=adapter_up_weight, member=member)


adapter_scale = 2.0
contract_trailing = (((1,), (1,)), ((), ()))
contract_leading = (((0,), (0,)), ((), ()))


def reference(tokens, cotangent, frozen_value_weight, adapter_down_weight, adapter_up_weight, member):
    feature_width = MODEL_WIDTH // N_TENSOR
    slice_weights = frozen_value_weight.reshape(N_TENSOR, feature_width, VALUE_FEATURES)
    group_tokens = tokens.reshape(N_DP, ROWS, MODEL_WIDTH)
    group_cot = cotangent.reshape(N_DP, ROWS, VALUE_FEATURES)
    group_ids = member.reshape(N_DP, NB).astype(jnp.int32)

    def group_step(totals, group_item):
        these_tokens, these_cot, these_ids = group_item
        sliced = these_tokens.reshape(ROWS, N_TENSOR, feature_width).transpose(1, 0, 2)

        def add_slice(running, paired):
            feature_piece, weight_piece = paired
            partial_sum = jnp.dot(feature_piece, weight_piece, preferred_element_type=jnp.float32).astype(jnp.bfloat16)
            partial_sum = lax.optimization_barrier(partial_sum)
            return running + partial_sum.astype(jnp.float32), None

        base_total, _ = lax.scan(add_slice, jnp.zeros((ROWS, VALUE_FEATURES), jnp.float32), (sliced, slice_weights))
        block_tokens = these_tokens.reshape(NB, BLK, MODEL_WIDTH)
        block_cots = these_cot.reshape(NB, BLK, VALUE_FEATURES)

        def block_step(grads, block_item):
            grad_a, grad_b = grads
            block_rows, block_cotangent, current_member = block_item
            down_projection = adapter_down_weight[current_member]
            up_projection = adapter_up_weight[current_member]
            hidden_state = lax.dot_general(block_rows, down_projection, contract_trailing, preferred_element_type=jnp.float32).astype(jnp.bfloat16)
            adapter_result = (adapter_scale * jnp.dot(hidden_state, up_projection, preferred_element_type=jnp.float32)).astype(jnp.bfloat16)
            backward_projection = (adapter_scale * lax.dot_general(block_cotangent, up_projection, contract_trailing, preferred_element_type=jnp.float32)).astype(jnp.bfloat16)
            term_down = lax.dot_general(backward_projection, block_rows, contract_leading, preferred_element_type=jnp.float32)
            up_term_value = adapter_scale * lax.dot_general(hidden_state, block_cotangent, contract_leading, preferred_element_type=jnp.float32)
            grad_a = grad_a.at[current_member].add(term_down)
            grad_b = grad_b.at[current_member].add(up_term_value)
            return (grad_a, grad_b), adapter_result

        start_grads = (jnp.zeros((MEMBER_COUNT, ADAPTER_RANK, MODEL_WIDTH), jnp.float32), jnp.zeros((MEMBER_COUNT, ADAPTER_RANK, VALUE_FEATURES), jnp.float32))
        (group_down, group_up), outs = lax.scan(block_step, start_grads, (block_tokens, block_cots, these_ids))
        output_rows = (base_total + outs.reshape(ROWS, VALUE_FEATURES).astype(jnp.float32)).astype(jnp.bfloat16)
        round_down = lax.optimization_barrier(group_down.astype(jnp.bfloat16))
        round_up = lax.optimization_barrier(group_up.astype(jnp.bfloat16))
        totals = (totals[0] + round_down.astype(jnp.float32), totals[1] + round_up.astype(jnp.float32))
        return totals, output_rows

    start_totals = (jnp.zeros((MEMBER_COUNT, ADAPTER_RANK, MODEL_WIDTH), jnp.float32), jnp.zeros((MEMBER_COUNT, ADAPTER_RANK, VALUE_FEATURES), jnp.float32))
    (grad_down, grad_up), outputs = lax.scan(group_step, start_totals, (group_tokens, group_cot, group_ids))
    return outputs.reshape(TOKENS, VALUE_FEATURES), grad_down, grad_up
```

```python
import functools

import jax
import jax.numpy as jnp
from jax import lax
from jax.experimental import pallas as pl
from jax.experimental.pallas import tpu as pltpu
from jax.sharding import PartitionSpec as P

BLK = 128
SCALE = 2.0
TRAIL = (((1,), (1,)), ((), ()))
LEAD = (((0,), (0,)), ((), ()))
F32 = jnp.float32
BF16 = jnp.bfloat16


def levels_of(nz):
    return [1 << l for l in range(nz.bit_length() - 1)]


def each(lo, hi, fn):
    if hi - lo <= 16:
        for k in range(lo, hi):
            fn(k)
    else:
        def step(k, c):
            fn(k)
            return c
        lax.fori_loop(lo, hi, step, 0)


def kernel(n, dp, member, tok_h, cot_h, w_h, down_h, up_h, out_h, gr, ur,
           tok, cot, w, dw, uc, uw, bs, bx, bn, acc, out, sel, sb, rb, sh, rh, ball, hall, gm, gs, gx, ad,
           us, ux, in_s, oc_s, uc_s, uc_r, wd_s, wd_r, wy_s, wy_r, wm_s, wm_r, wn_s, wn_r, uw_s, uw_r, um_s, um_r,
           bx_s, bx_r, bn_s, bn_r, rb_s, rb_r, ab_s, ab_r, rh_s, rh_r, ah_s, ah_r, gx_s, gx_r, g_s, g_r,
           ux_s, ux_r, u_s, u_r):
    d = lax.axis_index("dp")
    j = lax.axis_index("tensor")
    total = dp * n
    lin = d * n + j
    rows, feat = tok.shape
    part_rows = rows // n
    width = w.shape[1]
    rank = dw.shape[1]
    chunk = cot.shape[0]
    cw = cot_h.shape[0]
    share = chunk // cw
    half = rank // 2
    per = n // dp
    nz = n // 2
    ny = dp // 2
    blocks = rows // BLK
    core = d % 2
    mate = d + 1 - 2 * core
    ybit = (d // 2) % 2
    ymate = d + 2 - 4 * ybit
    px = j % 2
    zme = j // 2
    partner = j + 1 - 2 * px
    mine = pl.ds(pl.multiple_of(core * half, half), half)
    other = pl.ds(pl.multiple_of((1 - core) * half, half), half)
    fh = feat // 2
    cols = pl.ds(pl.multiple_of(ybit * fh, fh), fh)
    ycols = pl.ds(pl.multiple_of((1 - ybit) * fh, fh), fh)

    def rcopy(src, dst, s, r, dd, tt):
        return pltpu.make_async_remote_copy(
            src_ref=src, dst_ref=dst, send_sem=s, recv_sem=r,
            device_id={"dp": dd, "tensor": tt}, device_id_type=pl.DeviceIdType.MESH)

    def peer(o):
        return (j + o) % n

    def source(o):
        return (j + n - o) % n

    def block_owner(k):
        return (k * n) // blocks

    my_block = (j * blocks + n - 1) // n
    reduces = jnp.logical_and(my_block < blocks, (my_block * n) // blocks == j)
    block_at = jnp.minimum(my_block, blocks - 1)

    barrier = pltpu.get_barrier_semaphore()

    def greet(o):
        t = (lin + o) % total
        pl.semaphore_signal(barrier, inc=1, device_id={"dp": t // n, "tensor": t % n},
                            device_id_type=pl.DeviceIdType.MESH)

    cot[...] = jnp.zeros_like(cot)
    loads = [pltpu.make_async_copy(a, b, in_s.at[k]) for k, (a, b) in enumerate((
        (w_h, w), (tok_h, tok),
        (cot_h, cot.at[pl.ds(pl.multiple_of((j % share) * cw, cw), cw)]),
        (up_h.at[:, pl.ds(pl.multiple_of((j // share) * chunk, chunk), chunk)], uc.at[j]),
        (down_h.at[:, pl.ds(pl.multiple_of(j * feat, feat), feat)], dw.at[j]),
        (up_h, uw.at[j])))]
    for one in loads:
        one.start()
    each(1, total, greet)
    loads[0].wait()
    loads[1].wait()

    if part_rows % 16 == 0:
        def base(i):
            x = tok[pl.ds(pl.multiple_of(i * part_rows, 16), part_rows), :]
            bs[i] = jnp.dot(x, w[...], preferred_element_type=F32).astype(BF16)
    else:
        def whole(k):
            at = pl.ds(pl.multiple_of(k * BLK, BLK), BLK)
            acc[at, :] = jnp.dot(tok[at, :], w[...], preferred_element_type=F32)

        each(0, blocks, whole)

        def base(i):
            bs[i] = acc[pl.ds(pl.multiple_of(i * part_rows, 8), part_rows), :].astype(BF16)

    masks = levels_of(nz)
    starts = [nz - nz // m for m in masks]
    order = [sum(m for m, b in zip(masks, reversed(masks)) if q & b) for q in range(nz)][::-1]

    def far(q):
        return zme ^ order[q]

    def bx_copy(q):
        z = far(q)
        return rcopy(bs.at[2 * z + 1 - px], bx.at[z], bx_s.at[z], bx_r.at[z], d, partner)

    base(2 * far(0) + 1 - px)
    pl.semaphore_wait(barrier, total - 1)

    def uc_copy(o):
        t = peer(o)
        return rcopy(up_h.at[:, pl.ds(pl.multiple_of((t // share) * chunk, chunk), chunk)], uc.at[j],
                     uc_s.at[o], uc_r.at[o], d, t)

    def down_copy(o):
        t = peer(o)
        return rcopy(down_h.at[mine, pl.ds(pl.multiple_of(t * feat + ybit * fh, fh), fh)], dw.at[j, mine, cols],
                     wd_s.at[o], wd_r.at[o], d, t)

    def up_copy(o):
        return rcopy(up_h.at[mine], uw.at[j, mine], uw_s.at[o], uw_r.at[o], d, peer(o))

    each(1, n, lambda o: uc_copy(o).start())
    each(1, n, lambda o: down_copy(o).start())
    bx_copy(0).start()
    each(1, nz, lambda q: base(2 * far(q) + 1 - px))
    each(0, nz, lambda q: base(2 * far(q) + px))

    def got(ref, at, r, o):
        s = source(o)
        rcopy(ref.at[at(s)], ref.at[at(s)], r.at[o], r.at[o], d, s).wait_recv()

    for one in loads[2:]:
        one.wait()

    def reduce_send(send, recv, s_sem, r_sem):
        def start(k):
            @pl.when(block_owner(k) != j)
            def _():
                rcopy(send.at[k], recv.at[j], s_sem.at[k], r_sem.at[j], d, block_owner(k)).start()
        each(0, blocks, start)

        @pl.when(reduces)
        def _():
            recv[j] = send[block_at]

    def reduce_drain(send, recv, s_sem, r_sem):
        def wait(k):
            @pl.when(block_owner(k) != j)
            def _():
                rcopy(send.at[k], recv.at[j], s_sem.at[k], r_sem.at[j], d, block_owner(k)).wait_send()
        each(0, blocks, wait)

    def spread_copy(full, s_sem, r_sem, o):
        return rcopy(full.at[block_at], full.at[block_at], s_sem.at[o], r_sem.at[block_at], d, peer(o))

    def reduce_join(recv, r_sem, full, as_sem, ar_sem):
        @pl.when(reduces)
        def _():
            def wait(o):
                s = source(o)
                rcopy(recv.at[s], recv.at[s], r_sem.at[s], r_sem.at[s], d, s).wait_recv()
            each(1, n, wait)
            full[block_at] = sum(recv[s].astype(F32) for s in range(n)).astype(BF16)
            each(1, n, lambda o: spread_copy(full, as_sem, ar_sem, o).start())

    def spread_wait(full, r_sem):
        def wait(k):
            @pl.when(block_owner(k) != j)
            def _():
                rcopy(full.at[k], full.at[k], r_sem.at[k], r_sem.at[k], d, block_owner(k)).wait_recv()
        each(0, blocks, wait)

    def spread_drain(full, s_sem, r_sem):
        @pl.when(reduces)
        def _():
            each(1, n, lambda o: spread_copy(full, s_sem, r_sem, o).wait_send())

    group = blocks if blocks <= 8 else (2 if blocks % 2 == 0 else 1)

    def pick(dest, make, scale):
        def step(g):
            at = pl.ds(pl.multiple_of(g * group * BLK, BLK), group * BLK)
            sel[...] = (scale * make(at)).reshape(n, rank, group * BLK)
            for i in range(group):
                k = g * group + i
                dest[k] = sel[member[k], :, i * BLK:(i + 1) * BLK].astype(BF16)
        each(0, blocks // group, step)

    each(1, n, lambda o: got(uc, lambda s: s, uc_r, o))
    upall = uc[...].reshape(n * rank, chunk)
    pick(sb, lambda at: jnp.dot(upall, cot[:, at], preferred_element_type=F32), SCALE)
    reduce_send(sb, rb, rb_s, rb_r)
    each(1, 2, lambda q: bx_copy(q).start())
    each(1, n, lambda o: up_copy(o).start())

    def dw_y(o):
        s = source(o)
        return rcopy(dw.at[s, mine, cols], dw.at[s, mine, cols], wy_s.at[o], wy_r.at[o], ymate, j)

    def dw_mate(o):
        s = source(o)
        return rcopy(dw.at[s, mine, cols], dw.at[s, mine, cols], wm_s.at[o], wm_r.at[o], mate, j)

    def dw_mate_y(o):
        s = source(o)
        return rcopy(dw.at[s, mine, ycols], dw.at[s, mine, ycols], wn_s.at[o], wn_r.at[o], mate, j)

    def dw_got(o):
        s = source(o)
        rcopy(dw.at[s, mine, cols], dw.at[s, mine, cols], wd_s.at[o], wd_r.at[o], d, s).wait_recv()
        dw_y(o).start()
        dw_mate(o).start()

    each(1, n, dw_got)
    reduce_join(rb, rb_r, ball, ab_s, ab_r)

    def kept(z, m, u):
        return (z % (2 * m)) + u * 2 * m

    def bn_copy(l, u):
        m = masks[l]
        z = zme ^ m
        t = 2 * kept(z, m, u) + px
        return rcopy(bs.at[t], bn.at[starts[l] + u], bn_s.at[starts[l] + u], bn_r.at[starts[l] + u], d, 2 * z + px)

    def base_join(q):
        z = far(q)
        bx_copy(q).wait_recv()
        i = 2 * z + px
        bs[i] = (bs[i].astype(F32) + bx[z].astype(F32)).astype(BF16)

    each(2, nz, lambda q: bx_copy(q).start())
    each(0, nz, base_join)
    bn_copy(0, 0).start()
    each(1, nz // 2, lambda u: bn_copy(0, u).start())

    def dw_next(o):
        s = source(o)
        rcopy(dw.at[s, mine, ycols], dw.at[s, mine, ycols], wy_s.at[o], wy_r.at[o], ymate, j).wait_recv()
        dw_mate_y(o).start()

    each(1, n, dw_next)

    def up_mate(o):
        s = source(o)
        return rcopy(uw.at[s, mine], uw.at[s, mine], um_s.at[o], um_r.at[o], mate, j)

    def up_got(o):
        s = source(o)
        rcopy(uw.at[s, mine], uw.at[s, mine], uw_s.at[o], uw_r.at[o], d, s).wait_recv()
        up_mate(o).start()

    each(1, n, up_got)

    def dw_done(o):
        s = source(o)
        rcopy(dw.at[s, other, cols], dw.at[s, other, cols], wm_s.at[o], wm_r.at[o], mate, j).wait_recv()
        rcopy(dw.at[s, other, ycols], dw.at[s, other, ycols], wn_s.at[o], wn_r.at[o], mate, j).wait_recv()

    each(1, n, dw_done)
    downall = dw[...].reshape(n * rank, feat)
    pick(sh, lambda at: lax.dot_general(downall, tok[at, :], TRAIL, preferred_element_type=F32), 1.0)
    reduce_send(sh, rh, rh_s, rh_r)

    def masked(full):
        owner_row = lax.broadcasted_iota(jnp.int32, (n * rank, BLK), 0) // rank
        for k in range(blocks):
            tiled = jnp.concatenate([full[k]] * n, axis=0)
            gm[:, k * BLK:(k + 1) * BLK] = jnp.where(owner_row == member[k], tiled, jnp.zeros_like(tiled))

    def grads_of(lo):
        part = gm[pl.ds(pl.multiple_of(lo * rank, nz * rank), nz * rank), :]
        g = jnp.dot(part, tok[...], preferred_element_type=F32)
        return g.astype(BF16).reshape(nz, rank, feat)

    def gx_copy(k):
        return rcopy(gs.at[k], gx.at[k], gx_s.at[k], gx_r.at[k], mate, j)

    spread_wait(ball, ab_r)
    masked(ball)
    gs[0:nz] = grads_of((1 - core) * nz)
    each(0, nz, lambda k: gx_copy(k).start())
    gs[nz:n] = grads_of(core * nz)

    dd, slot = j // per, (d // 2) * per + j % per

    def gd_copy(k):
        return rcopy(gs.at[nz + k], gr.at[slot], g_s.at[k], g_r.at[slot], dd, core * nz + k)

    def not_me(k):
        return jnp.logical_or(dd != d, core * nz + k != j)

    def gd_start(k):
        gx_copy(k).wait_recv()
        gs[nz + k] = (gs[nz + k].astype(F32) + gx[k].astype(F32)).astype(BF16)

        @pl.when(not_me(k))
        def _():
            gd_copy(k).start()

    reduce_join(rh, rh_r, hall, ah_s, ah_r)
    each(0, nz, gd_start)

    own_gd = jnp.logical_and(dd == d, j // nz == core)

    def own_copy():
        return pltpu.make_async_copy(gs.at[nz + j % nz], gr.at[slot], oc_s.at[0])

    @pl.when(own_gd)
    def _():
        own_copy().start()

    def bn_wait(l, u):
        m = masks[l]
        z = zme ^ m
        at = starts[l] + u
        rcopy(bn.at[at], bn.at[at], bn_s.at[at], bn_r.at[at], d, 2 * z + px).wait_recv()
        t = 2 * kept(zme, m, u) + px
        bs[t] = (bs[t].astype(F32) + bn[at].astype(F32)).astype(BF16)

    for l in range(len(masks)):
        if l > 0:
            each(0, nz // (2 * masks[l]), lambda u: bn_copy(l, u).start())
        if l < len(masks) - 1:
            each(0, nz // (2 * masks[l]), lambda u: bn_wait(l, u))

    spread_wait(hall, ah_r)
    masked(hall)
    gu = SCALE * lax.dot_general(gm[...], cot[...], TRAIL, preferred_element_type=F32)
    gu = gu.reshape(n, rank, chunk)
    part = rank // dp
    for k in range(dp):
        us[k % 2, :, k // 2] = gu[:, k * part:(k + 1) * part, :]

    ux_copy = rcopy(us.at[1 - core], ux, ux_s, ux_r, mate, j)
    ux_copy.start()

    each(1, n, lambda o: rcopy(uw.at[source(o), other], uw.at[source(o), other], um_s.at[o], um_r.at[o], mate, j).wait_recv())
    k0 = (j * part_rows) // BLK
    k1 = (j * part_rows + part_rows - 1) // BLK
    ad[0:BLK] = lax.dot_general(hall[k0], uw[member[k0]], LEAD, preferred_element_type=F32)
    ad[BLK:2 * BLK] = lax.dot_general(hall[k1], uw[member[k1]], LEAD, preferred_element_type=F32)

    ux_copy.wait_recv()
    us[core] = us[core] + ux[...]

    def gu_copy(o):
        e = (zme_lin + o) % (ny * n)
        return rcopy(us.at[core, e % n, e // n], ur.at[d // 2, j], u_s.at[o], u_r.at[o],
                     2 * (e // n) + core, e % n)

    zme_lin = (d // 2) * n + j
    each(1, ny * n, lambda o: gu_copy(o).start())
    own_u = pltpu.make_async_copy(us.at[core, j, d // 2], ur.at[d // 2, j], oc_s.at[1])
    own_u.start()

    last = len(masks) - 1
    at = starts[last]
    rcopy(bn.at[at], bn.at[at], bn_s.at[at], bn_r.at[at], d, 2 * (zme ^ masks[last]) + px).wait_recv()
    adapter = (SCALE * ad[pl.ds(pl.multiple_of(j * part_rows - k0 * BLK, 8), part_rows), :]).astype(BF16)
    out[...] = (bs[j].astype(F32) + bn[at].astype(F32) + adapter.astype(F32)).astype(BF16)
    out_copy = pltpu.make_async_copy(out, out_h, oc_s.at[2])
    out_copy.start()

    def gd_recv(k):
        sd, sj = 2 * (k // per) + j // nz, d * per + k % per

        @pl.when(jnp.logical_or(sd != d, sj != j))
        def _():
            rcopy(gr.at[k], gr.at[k], g_s.at[0], g_r.at[k], sd, sj).wait_recv()

    each(0, ny * per, gd_recv)

    def gu_recv(o):
        s = (zme_lin + ny * n - o) % (ny * n)
        rcopy(ur.at[s // n, s % n], ur.at[s // n, s % n], u_s.at[o], u_r.at[o], 2 * (s // n) + core, s % n).wait_recv()

    each(1, ny * n, gu_recv)
    own_u.wait()
    out_copy.wait()

    @pl.when(own_gd)
    def _():
        own_copy().wait()

    def drain(o):
        uc_copy(o).wait_send()
        down_copy(o).wait_send()
        up_copy(o).wait_send()
        dw_y(o).wait_send()
        dw_mate(o).wait_send()
        dw_mate_y(o).wait_send()
        up_mate(o).wait_send()

    each(1, n, drain)
    reduce_drain(sb, rb, rb_s, rb_r)
    reduce_drain(sh, rh, rh_s, rh_r)
    spread_drain(ball, ab_s, ab_r)
    spread_drain(hall, ah_s, ah_r)

    def drain_pair(z):
        bx_copy(z).wait_send()
        gx_copy(z).wait_send()

        @pl.when(not_me(z))
        def _():
            gd_copy(z).wait_send()

    each(0, nz, drain_pair)
    for l in range(len(masks)):
        each(0, nz // (2 * masks[l]), lambda u: bn_copy(l, u).wait_send())
    ux_copy.wait_send()
    each(1, ny * n, lambda o: gu_copy(o).wait_send())


def tail(per, share, out_in, gr, ur, out, gdown, gup):
    out[...] = out_in[...]
    ny, n = ur.shape[:2]
    feat, chunk = gr.shape[2], ur.shape[3]
    for q in range(per):
        gdown[:, q * feat:(q + 1) * feat] = sum(gr[k * per + q].astype(F32) for k in range(ny))
    for c in range(n // share):
        gup[:, c * chunk:(c + 1) * chunk] = sum(
            ur[y, c * share + i] for y in range(ny) for i in range(share))


def solution(mesh):
    dp, n = mesh.shape["dp"], mesh.shape["tensor"]

    def shards(tokens, cotangent, w, down, up, member):
        rows, feat = tokens.shape
        cw, width, rank = cotangent.shape[1], w.shape[1], up.shape[1]
        per, nz, ny = n // dp, n // 2, dp // 2
        part_rows, blocks = rows // n, rows // BLK
        chunk = max(cw, 128)
        group = blocks if blocks <= 8 else (2 if blocks % 2 == 0 else 1)
        vmem = pl.BlockSpec(memory_space=pltpu.VMEM)
        anywhere = pl.BlockSpec(memory_space=pl.ANY)
        dma = lambda k: pltpu.SemaphoreType.DMA((k,))
        plain = part_rows % 16 == 0
        parts = pl.pallas_call(
            functools.partial(kernel, n, dp),
            out_shape=(
                jax.ShapeDtypeStruct((part_rows, width), BF16),
                jax.ShapeDtypeStruct((ny * per, rank, feat), BF16),
                jax.ShapeDtypeStruct((ny, n, rank // dp, chunk), F32),
            ),
            in_specs=[pl.BlockSpec(memory_space=pltpu.SMEM)] + [anywhere] * 5,
            out_specs=(anywhere,) * 3,
            scratch_shapes=[
                pltpu.VMEM((rows, feat), BF16),
                pltpu.VMEM((chunk, rows), BF16),
                pltpu.VMEM((feat, width), BF16),
                pltpu.VMEM((n, rank, feat), BF16),
                pltpu.VMEM((n, rank, chunk), BF16),
                pltpu.VMEM((n, rank, width), BF16),
                pltpu.VMEM((n, part_rows, width), BF16),
                pltpu.VMEM((nz, part_rows, width), BF16),
                pltpu.VMEM((nz, part_rows, width), BF16),
                pltpu.VMEM((8, 128) if plain else (rows, width), F32),
                pltpu.VMEM((part_rows, width), BF16),
                pltpu.VMEM((n, rank, group * BLK), F32),
                pltpu.VMEM((blocks, rank, BLK), BF16),
                pltpu.VMEM((n, rank, BLK), BF16),
                pltpu.VMEM((blocks, rank, BLK), BF16),
                pltpu.VMEM((n, rank, BLK), BF16),
                pltpu.VMEM((blocks, rank, BLK), BF16),
                pltpu.VMEM((blocks, rank, BLK), BF16),
                pltpu.VMEM((n * rank, rows), BF16),
                pltpu.VMEM((n, rank, feat), BF16),
                pltpu.VMEM((nz, rank, feat), BF16),
                pltpu.VMEM((2 * BLK, width), F32),
                pltpu.VMEM((2, n, ny, rank // dp, chunk), F32),
                pltpu.VMEM((n, ny, rank // dp, chunk), F32),
                dma(6), dma(3),
                *[dma(n) for _ in range(14)],
                dma(nz), dma(nz), dma(nz), dma(nz),
                *[dma(n) for _ in range(8)],
                dma(nz), dma(nz), dma(nz), dma(ny * per),
                pltpu.SemaphoreType.DMA, pltpu.SemaphoreType.DMA,
                dma(ny * n), dma(ny * n),
            ],
            compiler_params=pltpu.CompilerParams(
                collective_id=0, has_side_effects=True, vmem_limit_bytes=56 * 1024 * 1024),
        )(member[:, 0], tokens, cotangent.T, w, down[0], up[0])
        out, gdown, gup = pl.pallas_call(
            functools.partial(tail, per, chunk // cw),
            out_shape=(
                jax.ShapeDtypeStruct((part_rows, width), BF16),
                jax.ShapeDtypeStruct((rank, per * feat), F32),
                jax.ShapeDtypeStruct((rank // dp, width), F32),
            ),
            in_specs=[vmem] * 3,
            out_specs=(vmem,) * 3,
        )(*parts)
        return out, gdown[None], gup[None]

    return jax.shard_map(
        shards,
        mesh=mesh,
        in_specs=(P("dp", "tensor"), P("dp", "tensor"), P("tensor", None), P("tensor", None, None),
                  P("tensor", None, None), P("dp", None)),
        out_specs=(P(("dp", "tensor"), None), P("tensor", None, "dp"), P("tensor", "dp", None)),
        check_vma=False,
    )
```

```python
import functools

import jax
import jax.numpy as jnp
from jax import lax
from jax.experimental import pallas as pl
from jax.experimental.pallas import tpu as pltpu
from jax.sharding import PartitionSpec as P

BLK = 128
SCALE = 2.0
TRAIL = (((1,), (1,)), ((), ()))
LEAD = (((0,), (0,)), ((), ()))
F32 = jnp.float32
BF16 = jnp.bfloat16


def levels_of(nz):
    return [1 << l for l in range(nz.bit_length() - 1)]


def each(lo, hi, fn):
    if hi - lo <= 16:
        for k in range(lo, hi):
            fn(k)
    else:
        def step(k, c):
            fn(k)
            return c
        lax.fori_loop(lo, hi, step, 0)


def kernel(n, dp, member, tok_h, cot_h, w_h, down_h, up_h, out_h, gr, ur,
           tok, cot, w, dw, uc, uw, bs, bx, bn, acc, out, sel, sb, rb, sh, rh, ball, hall, gm, gs, gx, ad,
           us, ux, in_s, oc_s, uc_s, uc_r, wd_s, wd_r, wy_s, wy_r, wm_s, wm_r, uw_s, uw_r, um_s, um_r,
           bx_s, bx_r, bn_s, bn_r, rb_s, rb_r, ab_s, ab_r, rh_s, rh_r, ah_s, ah_r, gx_s, gx_r, g_s, g_r,
           ux_s, ux_r, u_s, u_r):
    d = lax.axis_index("dp")
    j = lax.axis_index("tensor")
    total = dp * n
    lin = d * n + j
    rows, feat = tok.shape
    part_rows = rows // n
    rank = dw.shape[1]
    chunk = cot.shape[0]
    cw = cot_h.shape[0]
    share = chunk // cw
    half = rank // 2
    per = n // dp
    nz = n // 2
    ny = dp // 2
    blocks = rows // BLK
    core = d % 2
    mate = d + 1 - 2 * core
    ybit = (d // 2) % 2
    ymate = d + 2 - 4 * ybit
    px = j % 2
    zme = j // 2
    partner = j + 1 - 2 * px
    mine = pl.ds(pl.multiple_of(core * half, half), half)
    fh = feat // 2
    cols = pl.ds(pl.multiple_of(ybit * fh, fh), fh)
    ycols = pl.ds(pl.multiple_of((1 - ybit) * fh, fh), fh)
    side = j // nz

    def rcopy(src, dst, s, r, dd, tt):
        return pltpu.make_async_remote_copy(
            src_ref=src, dst_ref=dst, send_sem=s, recv_sem=r,
            device_id={"dp": dd, "tensor": tt}, device_id_type=pl.DeviceIdType.MESH)

    def received(ref, sem):
        rcopy(ref, ref, sem, sem, d, partner).wait_recv()

    def sent(ref, sem):
        rcopy(ref, ref, sem, sem, d, partner).wait_send()

    def peer(o):
        return (j + o) % n

    def block_owner(k):
        return (k * n) // blocks

    my_block = (j * blocks + n - 1) // n
    reduces = jnp.logical_and(my_block < blocks, (my_block * n) // blocks == j)
    block_at = jnp.minimum(my_block, blocks - 1)

    barrier = pltpu.get_barrier_semaphore()

    def greet(o):
        t = (lin + o) % total
        pl.semaphore_signal(barrier, inc=1, device_id={"dp": t // n, "tensor": t % n},
                            device_id_type=pl.DeviceIdType.MESH)

    each(1, total, greet)
    cot[...] = jnp.zeros_like(cot)
    loads = [pltpu.make_async_copy(a, b, in_s.at[k]) for k, (a, b) in enumerate((
        (w_h, w), (tok_h, tok),
        (cot_h, cot.at[pl.ds(pl.multiple_of((j % share) * cw, cw), cw)]),
        (up_h.at[:, pl.ds(pl.multiple_of((j // share) * chunk, chunk), chunk)], uc.at[j]),
        (down_h.at[mine, pl.ds(pl.multiple_of(j * feat + ybit * fh, fh), fh)], dw.at[j, mine, cols]),
        (up_h.at[mine], uw.at[j, mine])))]
    for one in loads:
        one.start()
    loads[0].wait()
    loads[1].wait()

    if part_rows % 16 == 0:
        def base(i):
            x = tok[pl.ds(pl.multiple_of(i * part_rows, 16), part_rows), :]
            bs[i] = jnp.dot(x, w[...], preferred_element_type=F32).astype(BF16)
    else:
        def whole(k):
            at = pl.ds(pl.multiple_of(k * BLK, BLK), BLK)
            acc[at, :] = jnp.dot(tok[at, :], w[...], preferred_element_type=F32)

        each(0, blocks, whole)

        def base(i):
            bs[i] = acc[pl.ds(pl.multiple_of(i * part_rows, 8), part_rows), :].astype(BF16)

    masks = levels_of(nz)
    starts = [nz - nz // m for m in masks]

    def bx_copy(v):
        z = zme ^ v
        return rcopy(bs.at[2 * z + 1 - px], bx.at[v], bx_s.at[0], bx_r.at[v], d, partner)

    def base_far(v):
        base(2 * (zme ^ v) + 1 - px)

    def base_own(v):
        base(2 * (zme ^ v) + px)

    def bn_copy(l, c):
        m = masks[l]
        at = starts[l] + c // (2 * m)
        return rcopy(bs.at[2 * (zme ^ m ^ c) + px], bn.at[at], bn_s.at[0], bn_r.at[at], d, 2 * (zme ^ m) + px)

    def bx_step(v):
        received(bx.at[v], bx_r.at[v])
        i = 2 * (zme ^ v) + px
        bs[i] = (bs[i].astype(F32) + bx[v].astype(F32)).astype(BF16)
        if v % 2:
            bn_copy(0, v - 1).start()

    def bn_step(l, c):
        at = starts[l] + c // (2 * masks[l])
        received(bn.at[at], bn_r.at[at])
        i = 2 * (zme ^ c) + px
        bs[i] = (bs[i].astype(F32) + bn[at].astype(F32)).astype(BF16)
        if c & masks[l + 1]:
            bn_copy(l + 1, c - masks[l + 1]).start()

    steps = []
    for v in range(nz - 1, -1, -1):
        steps.append(functools.partial(bx_step, v))
        if v % 2 and v + 1 < nz:
            steps.append(functools.partial(bn_step, 0, v + 1))
    steps.append(functools.partial(bn_step, 0, 0))
    for l in range(1, len(masks) - 1):
        for c in range(nz - 2 * masks[l], -1, -2 * masks[l]):
            steps.append(functools.partial(bn_step, l, c))

    def advance(k):
        for _ in range(min(k, len(steps))):
            steps.pop(0)()

    def uc_copy(o):
        t = peer(o)
        return rcopy(up_h.at[:, pl.ds(pl.multiple_of((t // share) * chunk, chunk), chunk)], uc.at[j],
                     uc_s.at[0], uc_r.at[0], d, t)

    def down_copy(o):
        t = peer(o)
        group = jnp.where(t // nz == side, 0, 1)
        return rcopy(down_h.at[mine, pl.ds(pl.multiple_of(t * feat + ybit * fh, fh), fh)], dw.at[j, mine, cols],
                     wd_s.at[0], wd_r.at[group], d, t)

    def slots(g):
        return pl.ds((side + g - 2 * side * g) * nz, nz)

    def dw_y(g):
        ref = dw.at[slots(g), mine, cols]
        return rcopy(ref, ref, wy_s.at[0], wy_r.at[g], ymate, j)

    def dw_mate(g, at, i):
        ref = dw.at[slots(g), mine, at]
        return rcopy(ref, ref, wm_s.at[0], wm_r.at[2 * i + g], mate, j)

    def up_copy(o):
        return rcopy(up_h.at[mine], uw.at[j, mine], uw_s.at[0], uw_r.at[0], d, peer(o))

    def up_mate():
        ref = uw.at[:, mine]
        return rcopy(ref, ref, um_s.at[0], um_r.at[0], mate, j)

    def reduce_send(send, recv, s_sem, r_sem):
        def start(k):
            @pl.when(block_owner(k) != j)
            def _():
                rcopy(send.at[k], recv.at[j], s_sem.at[0], r_sem.at[0], d, block_owner(k)).start()
        each(0, blocks, start)

        @pl.when(reduces)
        def _():
            recv[j] = send[block_at]

    def but_own(ref, count, own, wait, sem):
        @pl.when(own)
        def _():
            if count > 1:
                wait(ref.at[0:count - 1], sem)

        @pl.when(jnp.logical_not(own))
        def _():
            wait(ref.at[0:count], sem)

    def spread_copy(full, s_sem, r_sem, o):
        return rcopy(full.at[block_at], full.at[block_at], s_sem.at[0], r_sem.at[0], d, peer(o))

    def spread_send(recv, r_sem, full, s_sem, f_sem):
        @pl.when(reduces)
        def _():
            received(recv.at[0:n - 1], r_sem.at[0])
            full[block_at] = sum(recv[s].astype(F32) for s in range(n)).astype(BF16)
            each(1, n, lambda o: spread_copy(full, s_sem, f_sem, o).start())

    group = blocks if blocks <= 8 else (2 if blocks % 2 == 0 else 1)

    def pick(dest, make, scale):
        def step(g):
            at = pl.ds(pl.multiple_of(g * group * BLK, BLK), group * BLK)
            sel[...] = (scale * make(at)).reshape(n, rank, group * BLK)
            for i in range(group):
                k = g * group + i
                dest[k] = sel[member[k], :, i * BLK:(i + 1) * BLK].astype(BF16)
        each(0, blocks // group, step)

    def masked(full):
        owner_row = lax.broadcasted_iota(jnp.int32, (n * rank, BLK), 0) // rank
        for k in range(blocks):
            tiled = jnp.concatenate([full[k]] * n, axis=0)
            gm[:, k * BLK:(k + 1) * BLK] = jnp.where(owner_row == member[k], tiled, jnp.zeros_like(tiled))

    def grads_of(lo):
        part = gm[pl.ds(pl.multiple_of(lo * rank, nz * rank), nz * rank), :]
        g = jnp.dot(part, tok[...], preferred_element_type=F32)
        return g.astype(BF16).reshape(nz, rank, feat)

    gx_copy = rcopy(gs.at[0:nz], gx, gx_s, gx_r, mate, j)
    dd, slot = j // per, (d // 2) * per + j % per

    def gd_copy(k):
        return rcopy(gs.at[nz + k], gr.at[slot], g_s.at[0], g_r.at[0], dd, core * nz + k)

    own_gd = jnp.logical_and(dd == d, j // nz == core)

    def gd_step(k):
        gs[nz + k] = (gs[nz + k].astype(F32) + gx[k].astype(F32)).astype(BF16)

        @pl.when(jnp.logical_or(dd != d, core * nz + k != j))
        def _():
            gd_copy(k).start()

    def own_copy():
        return pltpu.make_async_copy(gs.at[nz + j % nz], gr.at[slot], oc_s.at[0])

    def own_start():
        @pl.when(own_gd)
        def _():
            own_copy().start()

    def own_wait():
        @pl.when(own_gd)
        def _():
            own_copy().wait()

    part = rank // dp

    def gu_make():
        gu = SCALE * lax.dot_general(gm[...], cot[...], TRAIL, preferred_element_type=F32)
        gu = gu.reshape(n, rank, chunk)
        for k in range(dp):
            us[k % 2, k // 2] = gu[:, k * part:(k + 1) * part, :]

    ux_copy = rcopy(us.at[1 - core], ux, ux_s, ux_r, mate, j)
    here = (d // 2) * n + j

    def gu_copy(o):
        e = (here + o) % (ny * n)
        return rcopy(us.at[core, e // n, e % n], ur.at[here], u_s.at[0], u_r.at[0],
                     2 * (e // n) + core, e % n)

    own_u = pltpu.make_async_copy(us.at[core, d // 2, j], ur.at[here], oc_s.at[1])
    out_copy = pltpu.make_async_copy(out, out_h, oc_s.at[2])
    k0 = (j * part_rows) // BLK
    k1 = (j * part_rows + part_rows - 1) // BLK

    def adapt():
        ad[0:BLK] = lax.dot_general(hall[k0], uw[member[k0]], LEAD, preferred_element_type=F32)
        ad[BLK:2 * BLK] = lax.dot_general(hall[k1], uw[member[k1]], LEAD, preferred_element_type=F32)

    def finish():
        adapter = (SCALE * ad[pl.ds(pl.multiple_of(j * part_rows - k0 * BLK, 8), part_rows), :]).astype(BF16)
        out[...] = (bs[j].astype(F32) + bn[starts[-1]].astype(F32) + adapter.astype(F32)).astype(BF16)

    base_far(nz - 1)
    pl.semaphore_wait(barrier, total - 1)

    each(1, n, lambda o: uc_copy(o).start())
    each(1, n, lambda o: down_copy(o).start())
    bx_copy(nz - 1).start()
    for v in range(nz - 2, -1, -1):
        base_far(v)
    for v in range(nz - 1, -1, -1):
        base_own(v)
    for one in loads[2:]:
        one.wait()
    received(uc.at[0:n - 1], uc_r.at[0])
    upall = uc[...].reshape(n * rank, chunk)
    pick(sb, lambda at: jnp.dot(upall, cot[:, at], preferred_element_type=F32), SCALE)
    reduce_send(sb, rb, rb_s, rb_r)
    bx_copy(nz - 2).start()
    each(1, n, lambda o: up_copy(o).start())
    for v in range(nz - 3, 0, -1):
        bx_copy(v).start()
    for g in range(2):
        received(dw.at[0:nz - 1 + g, 0:half, 0:fh], wd_r.at[g])
        dw_y(g).start()
        dw_mate(g, cols, 0).start()
    spread_send(rb, rb_r, ball, ab_s, ab_r)
    bx_copy(0).start()
    advance(1)
    for g in range(2):
        received(dw.at[0:nz, 0:half, 0:fh], wy_r.at[g])
        dw_mate(g, ycols, 1).start()
    advance(1)
    received(uw.at[0:n - 1, 0:half], uw_r.at[0])
    up_mate().start()
    for i in range(4):
        received(dw.at[0:nz, 0:half, 0:fh], wm_r.at[i])
    downall = dw[...].reshape(n * rank, feat)
    pick(sh, lambda at: lax.dot_general(downall, tok[at, :], TRAIL, preferred_element_type=F32), 1.0)
    reduce_send(sh, rh, rh_s, rh_r)
    advance(2)
    but_own(ball, blocks, reduces, received, ab_r.at[0])
    masked(ball)
    gs[0:nz] = grads_of((1 - core) * nz)
    gx_copy.start()
    gs[nz:n] = grads_of(core * nz)
    spread_send(rh, rh_r, hall, ah_s, ah_r)
    gx_copy.wait_recv()
    each(0, nz, gd_step)
    own_start()
    advance(len(steps))
    but_own(hall, blocks, reduces, received, ah_r.at[0])
    masked(hall)
    gu_make()
    ux_copy.start()
    received(uw.at[:, 0:half], um_r.at[0])
    adapt()
    ux_copy.wait_recv()
    us[core] = us[core] + ux[...]
    each(1, ny * n, lambda o: gu_copy(o).start())
    own_u.start()
    received(bn.at[starts[-1]], bn_r.at[starts[-1]])
    finish()
    out_copy.start()
    but_own(gr, ny * per, own_gd, received, g_r.at[0])
    received(ur.at[0:ny * n - 1], u_r.at[0])
    own_u.wait()
    out_copy.wait()
    own_wait()

    sent(uc.at[0:n - 1], uc_s.at[0])
    sent(dw.at[0:n - 1, 0:half, 0:fh], wd_s.at[0])
    sent(dw.at[:, 0:half, 0:fh], wy_s.at[0])
    sent(dw.at[:, 0:half], wm_s.at[0])
    sent(uw.at[0:n - 1, 0:half], uw_s.at[0])
    sent(uw.at[:, 0:half], um_s.at[0])
    but_own(sb, blocks, reduces, sent, rb_s.at[0])
    but_own(sh, blocks, reduces, sent, rh_s.at[0])

    @pl.when(reduces)
    def _():
        sent(rb.at[0:n - 1], ab_s.at[0])
        sent(rh.at[0:n - 1], ah_s.at[0])

    sent(bx, bx_s.at[0])
    sent(bn.at[0:nz - 1], bn_s.at[0])
    gx_copy.wait_send()
    but_own(gs, nz, own_gd, sent, g_s.at[0])
    ux_copy.wait_send()
    sent(ur.at[0:ny * n - 1], u_s.at[0])


def tail(per, share, out_in, gr, ur, out, gdown, gup):
    out[...] = out_in[...]
    ny = gr.shape[0] // per
    n = ur.shape[0] // ny
    feat, chunk = gr.shape[2], ur.shape[2]
    for q in range(per):
        gdown[:, q * feat:(q + 1) * feat] = sum(gr[k * per + q].astype(F32) for k in range(ny))
    for c in range(n // share):
        gup[:, c * chunk:(c + 1) * chunk] = sum(
            ur[y * n + c * share + i] for y in range(ny) for i in range(share))


def solution(mesh):
    dp, n = mesh.shape["dp"], mesh.shape["tensor"]

    def shards(tokens, cotangent, w, down, up, member):
        rows, feat = tokens.shape
        cw, width, rank = cotangent.shape[1], w.shape[1], up.shape[1]
        per, nz, ny = n // dp, n // 2, dp // 2
        part_rows, blocks = rows // n, rows // BLK
        chunk = max(cw, 128)
        group = blocks if blocks <= 8 else (2 if blocks % 2 == 0 else 1)
        vmem = pl.BlockSpec(memory_space=pltpu.VMEM)
        anywhere = pl.BlockSpec(memory_space=pl.ANY)
        dma = lambda k: pltpu.SemaphoreType.DMA((k,))
        plain = part_rows % 16 == 0
        parts = pl.pallas_call(
            functools.partial(kernel, n, dp),
            out_shape=(
                jax.ShapeDtypeStruct((part_rows, width), BF16),
                jax.ShapeDtypeStruct((ny * per, rank, feat), BF16),
                jax.ShapeDtypeStruct((ny * n, rank // dp, chunk), F32),
            ),
            in_specs=[pl.BlockSpec(memory_space=pltpu.SMEM)] + [anywhere] * 5,
            out_specs=(anywhere,) * 3,
            scratch_shapes=[
                pltpu.VMEM((rows, feat), BF16),
                pltpu.VMEM((chunk, rows), BF16),
                pltpu.VMEM((feat, width), BF16),
                pltpu.VMEM((n, rank, feat), BF16),
                pltpu.VMEM((n, rank, chunk), BF16),
                pltpu.VMEM((n, rank, width), BF16),
                pltpu.VMEM((n, part_rows, width), BF16),
                pltpu.VMEM((nz, part_rows, width), BF16),
                pltpu.VMEM((nz, part_rows, width), BF16),
                pltpu.VMEM((8, 128) if plain else (rows, width), F32),
                pltpu.VMEM((part_rows, width), BF16),
                pltpu.VMEM((n, rank, group * BLK), F32),
                pltpu.VMEM((blocks, rank, BLK), BF16),
                pltpu.VMEM((n, rank, BLK), BF16),
                pltpu.VMEM((blocks, rank, BLK), BF16),
                pltpu.VMEM((n, rank, BLK), BF16),
                pltpu.VMEM((blocks, rank, BLK), BF16),
                pltpu.VMEM((blocks, rank, BLK), BF16),
                pltpu.VMEM((n * rank, rows), BF16),
                pltpu.VMEM((n, rank, feat), BF16),
                pltpu.VMEM((nz, rank, feat), BF16),
                pltpu.VMEM((2 * BLK, width), F32),
                pltpu.VMEM((2, ny, n, rank // dp, chunk), F32),
                pltpu.VMEM((ny, n, rank // dp, chunk), F32),
                dma(6), dma(3),
                dma(1), dma(1), dma(1), dma(2), dma(1), dma(2), dma(1), dma(4), dma(1), dma(1), dma(1), dma(1),
                dma(1), dma(nz), dma(1), dma(nz), *[dma(1) for _ in range(8)],
                pltpu.SemaphoreType.DMA, pltpu.SemaphoreType.DMA, dma(1), dma(1),
                pltpu.SemaphoreType.DMA, pltpu.SemaphoreType.DMA, dma(1), dma(1),
            ],
            compiler_params=pltpu.CompilerParams(
                collective_id=0, has_side_effects=True, vmem_limit_bytes=56 * 1024 * 1024),
        )(member[:, 0], tokens, cotangent.T, w, down[0], up[0])
        out, gdown, gup = pl.pallas_call(
            functools.partial(tail, per, chunk // cw),
            out_shape=(
                jax.ShapeDtypeStruct((part_rows, width), BF16),
                jax.ShapeDtypeStruct((rank, per * feat), F32),
                jax.ShapeDtypeStruct((rank // dp, width), F32),
            ),
            in_specs=[vmem] * 3,
            out_specs=(vmem,) * 3,
        )(*parts)
        return out, gdown[None], gup[None]

    return jax.shard_map(
        shards,
        mesh=mesh,
        in_specs=(P("dp", "tensor"), P("dp", "tensor"), P("tensor", None), P("tensor", None, None),
                  P("tensor", None, None), P("dp", None)),
        out_specs=(P(("dp", "tensor"), None), P("tensor", None, "dp"), P("tensor", "dp", None)),
        check_vma=False,
    )
```

```python
import functools

import jax
import jax.numpy as jnp
from jax import lax
from jax.experimental import pallas as pl
from jax.experimental.pallas import tpu as pltpu
from jax.sharding import PartitionSpec as P

BLK = 128
SCALE = 2.0
TRAIL = (((1,), (1,)), ((), ()))
LEAD = (((0,), (0,)), ((), ()))
F32 = jnp.float32
BF16 = jnp.bfloat16


def levels_of(nz):
    return [1 << l for l in range(nz.bit_length() - 1)]


def each(lo, hi, fn):
    if hi - lo <= 16:
        for k in range(lo, hi):
            fn(k)
    else:
        def step(k, c):
            fn(k)
            return c
        lax.fori_loop(lo, hi, step, 0)


def kernel(n, dp, member, tok_h, cot_h, w_h, down_h, up_h, out_h, gr, ur,
           tok, cot, w, dw, uc, uw, bs, bx, bn, acc, out, sel, sb, rb, sh, rh, ball, hall, gm, gs, gx, ad,
           us, in_s, oc_s, uc_s, uc_r, wd_s, wd_r, wy_s, wy_r, wm_s, wm_r, uw_s, uw_r, um_s, um_r,
           bx_s, bx_r, bn_s, bn_r, rb_s, rb_r, ab_s, ab_r, rh_s, rh_r, ah_s, ah_r, gx_s, gx_r, g_s, g_r,
           u_s, u_r, fence):
    d = lax.axis_index("dp")
    j = lax.axis_index("tensor")
    rows, feat = tok.shape
    part_rows = rows // n
    rank = dw.shape[1]
    chunk = cot.shape[0]
    cw = cot_h.shape[0]
    share = chunk // cw
    half = rank // 2
    per = n // dp
    nz = n // 2
    ny = dp // 2
    blocks = rows // BLK
    core = d % 2
    mate = d + 1 - 2 * core
    ybit = (d // 2) % 2
    ymate = d + 2 - 4 * ybit
    px = j % 2
    zme = j // 2
    partner = j + 1 - 2 * px
    mine = pl.ds(pl.multiple_of(core * half, half), half)
    fh = feat // 2
    cols = pl.ds(pl.multiple_of(ybit * fh, fh), fh)
    ycols = pl.ds(pl.multiple_of((1 - ybit) * fh, fh), fh)
    side = j // nz

    def rcopy(src, dst, s, r, dd, tt):
        return pltpu.make_async_remote_copy(
            src_ref=src, dst_ref=dst, send_sem=s, recv_sem=r,
            device_id={"dp": dd, "tensor": tt}, device_id_type=pl.DeviceIdType.MESH)

    def received(ref, sem):
        rcopy(ref, ref, sem, sem, d, partner).wait_recv()

    def sent(ref, sem):
        rcopy(ref, ref, sem, sem, d, partner).wait_send()

    def peer(o):
        return (j + o) % n

    def block_owner(k):
        return (k * n) // blocks

    my_block = (j * blocks + n - 1) // n
    reduces = jnp.logical_and(my_block < blocks, (my_block * n) // blocks == j)
    block_at = jnp.minimum(my_block, blocks - 1)

    barrier = pltpu.get_barrier_semaphore()

    def signal(sem, dd, tt):
        pl.semaphore_signal(sem, inc=1, device_id={"dp": dd, "tensor": tt}, device_id_type=pl.DeviceIdType.MESH)

    each(1, n, lambda o: signal(barrier, d, peer(o)))
    each(1, dp, lambda o: signal(barrier, (d + o) % dp, j))
    cot[...] = jnp.zeros_like(cot)
    loads = [pltpu.make_async_copy(a, b, in_s.at[k]) for k, (a, b) in enumerate((
        (w_h, w), (tok_h, tok),
        (cot_h, cot.at[pl.ds(pl.multiple_of((j % share) * cw, cw), cw)]),
        (up_h.at[:, pl.ds(pl.multiple_of((j // share) * chunk, chunk), chunk)], uc.at[j]),
        (down_h.at[mine, pl.ds(pl.multiple_of(j * feat, feat), feat)], dw.at[j, mine]),
        (up_h.at[mine], uw.at[j, mine])))]
    for one in loads:
        one.start()
    loads[0].wait()
    loads[1].wait()

    if part_rows % 16 == 0:
        def base(i):
            x = tok[pl.ds(pl.multiple_of(i * part_rows, 16), part_rows), :]
            bs[i] = jnp.dot(x, w[...], preferred_element_type=F32).astype(BF16)
    else:
        def whole(k):
            at = pl.ds(pl.multiple_of(k * BLK, BLK), BLK)
            acc[at, :] = jnp.dot(tok[at, :], w[...], preferred_element_type=F32)

        each(0, blocks, whole)

        def base(i):
            bs[i] = acc[pl.ds(pl.multiple_of(i * part_rows, 8), part_rows), :].astype(BF16)

    masks = levels_of(nz)
    starts = [nz - nz // m for m in masks]

    def bx_copy(v):
        z = zme ^ v
        return rcopy(bs.at[2 * z + 1 - px], bx.at[v], bx_s.at[0], bx_r.at[v], d, partner)

    def base_far(v):
        base(2 * (zme ^ v) + 1 - px)

    def base_own(v):
        base(2 * (zme ^ v) + px)

    def bn_copy(l, c):
        m = masks[l]
        at = starts[l] + c // (2 * m)
        return rcopy(bs.at[2 * (zme ^ m ^ c) + px], bn.at[at], bn_s.at[0], bn_r.at[at], d, 2 * (zme ^ m) + px)

    def bx_step(v):
        received(bx.at[v], bx_r.at[v])
        i = 2 * (zme ^ v) + px
        bs[i] = (bs[i].astype(F32) + bx[v].astype(F32)).astype(BF16)
        if v % 2:
            bn_copy(0, v - 1).start()

    def bn_step(l, c):
        at = starts[l] + c // (2 * masks[l])
        received(bn.at[at], bn_r.at[at])
        i = 2 * (zme ^ c) + px
        bs[i] = (bs[i].astype(F32) + bn[at].astype(F32)).astype(BF16)
        if c & masks[l + 1]:
            bn_copy(l + 1, c - masks[l + 1]).start()

    steps = []
    for v in range(nz - 1, -1, -1):
        steps.append(functools.partial(bx_step, v))
        if v % 2 and v + 1 < nz:
            steps.append(functools.partial(bn_step, 0, v + 1))
    steps.append(functools.partial(bn_step, 0, 0))
    for l in range(1, len(masks) - 1):
        for c in range(nz - 2 * masks[l], -1, -2 * masks[l]):
            steps.append(functools.partial(bn_step, l, c))

    def advance(k):
        for _ in range(min(k, len(steps))):
            steps.pop(0)()

    def uc_copy(o):
        t = peer(o)
        return rcopy(up_h.at[:, pl.ds(pl.multiple_of((t // share) * chunk, chunk), chunk)], uc.at[j],
                     uc_s.at[0], uc_r.at[0], d, t)

    def near_copy(o):
        t = side * nz + (j + o) % nz
        return rcopy(down_h.at[mine, pl.ds(pl.multiple_of(t * feat, feat), feat)], dw.at[j, mine],
                     wd_s.at[0], wd_r.at[0], d, t)

    def far_copy(o):
        t = (1 - side) * nz + (j + o) % nz
        return rcopy(down_h.at[mine, pl.ds(pl.multiple_of(t * feat + ybit * fh, fh), fh)], dw.at[j, mine, cols],
                     wd_s.at[1], wd_r.at[1], d, t)

    near = pl.ds(side * nz, nz)
    distant = pl.ds((1 - side) * nz, nz)

    def dw_copy(slots, at, s_sem, r_sem, to):
        ref = dw.at[slots, mine, at]
        return rcopy(ref, ref, s_sem, r_sem, to, j)

    dw_y = dw_copy(distant, cols, wy_s.at[0], wy_r.at[0], ymate)
    dw_near = dw_copy(near, pl.ds(0, feat), wm_s.at[0], wm_r.at[0], mate)
    dw_far = dw_copy(distant, cols, wm_s.at[1], wm_r.at[1], mate)
    dw_next = dw_copy(distant, ycols, wm_s.at[1], wm_r.at[2], mate)

    def up_copy(o):
        return rcopy(up_h.at[mine], uw.at[j, mine], uw_s.at[0], uw_r.at[0], d, peer(o))

    def up_mate():
        ref = uw.at[:, mine]
        return rcopy(ref, ref, um_s.at[0], um_r.at[0], mate, j)

    def reduce_send(send, recv, s_sem, r_sem):
        def start(k):
            @pl.when(block_owner(k) != j)
            def _():
                rcopy(send.at[k], recv.at[j], s_sem.at[0], r_sem.at[0], d, block_owner(k)).start()
        each(0, blocks, start)

        @pl.when(reduces)
        def _():
            recv[j] = send[block_at]

    def but_own(ref, count, own, wait, sem):
        @pl.when(own)
        def _():
            if count > 1:
                wait(ref.at[0:count - 1], sem)

        @pl.when(jnp.logical_not(own))
        def _():
            wait(ref.at[0:count], sem)

    def spread_copy(full, s_sem, r_sem, o):
        return rcopy(full.at[block_at], full.at[block_at], s_sem.at[0], r_sem.at[0], d, peer(o))

    def spread_send(recv, r_sem, full, s_sem, f_sem):
        @pl.when(reduces)
        def _():
            received(recv.at[0:n - 1], r_sem.at[0])
            full[block_at] = sum(recv[s].astype(F32) for s in range(n)).astype(BF16)
            each(1, n, lambda o: spread_copy(full, s_sem, f_sem, o).start())

    group = blocks if blocks <= 8 else (2 if blocks % 2 == 0 else 1)

    def pick(dest, make, scale):
        def step(g):
            at = pl.ds(pl.multiple_of(g * group * BLK, BLK), group * BLK)
            sel[...] = (scale * make(at)).reshape(n, rank, group * BLK)
            for i in range(group):
                k = g * group + i
                dest[k] = sel[member[k], :, i * BLK:(i + 1) * BLK].astype(BF16)
        each(0, blocks // group, step)

    def masked(full):
        owner_row = lax.broadcasted_iota(jnp.int32, (n * rank, BLK), 0) // rank
        for k in range(blocks):
            tiled = jnp.concatenate([full[k]] * n, axis=0)
            gm[:, k * BLK:(k + 1) * BLK] = jnp.where(owner_row == member[k], tiled, jnp.zeros_like(tiled))

    def grads_of(lo):
        part = gm[pl.ds(pl.multiple_of(lo * rank, nz * rank), nz * rank), :]
        g = jnp.dot(part, tok[...], preferred_element_type=F32)
        return g.astype(BF16).reshape(nz, rank, feat)

    gx_copy = rcopy(gs.at[0:nz], gx, gx_s, gx_r, mate, j)
    dd, slot = j // per, (d // 2) * per + j % per

    def gd_copy(k):
        return rcopy(gs.at[nz + k], gr.at[slot], g_s.at[0], g_r.at[0], dd, core * nz + k)

    own_gd = jnp.logical_and(dd == d, j // nz == core)

    def gd_step(k):
        gs[nz + k] = (gs[nz + k].astype(F32) + gx[k].astype(F32)).astype(BF16)

        @pl.when(jnp.logical_or(dd != d, core * nz + k != j))
        def _():
            gd_copy(k).start()

    def own_copy():
        return pltpu.make_async_copy(gs.at[nz + j % nz], gr.at[slot], oc_s.at[0])

    def own_start():
        @pl.when(own_gd)
        def _():
            own_copy().start()

    def own_wait():
        @pl.when(own_gd)
        def _():
            own_copy().wait()

    part = rank // dp

    def gu_make():
        gu = SCALE * lax.dot_general(gm[...], cot[...], TRAIL, preferred_element_type=F32)
        gu = gu.reshape(n, rank, chunk)
        for k in range(dp):
            us[k] = gu[:, k * part:(k + 1) * part, :].astype(us.dtype)

    here = d * n + j

    def gu_copy(o):
        e = (here + o) % (dp * n)
        return rcopy(us.at[e // n, e % n], ur.at[here], u_s.at[0], u_r.at[0], e // n, e % n)

    own_u = pltpu.make_async_copy(us.at[d, j], ur.at[here], oc_s.at[1])
    out_copy = pltpu.make_async_copy(out, out_h, oc_s.at[2])
    k0 = (j * part_rows) // BLK
    k1 = (j * part_rows + part_rows - 1) // BLK

    def adapt():
        ad[0:BLK] = lax.dot_general(hall[k0], uw[member[k0]], LEAD, preferred_element_type=F32)
        ad[BLK:2 * BLK] = lax.dot_general(hall[k1], uw[member[k1]], LEAD, preferred_element_type=F32)

    def finish():
        adapter = (SCALE * ad[pl.ds(pl.multiple_of(j * part_rows - k0 * BLK, 8), part_rows), :]).astype(BF16)
        out[...] = (bs[j].astype(F32) + bn[starts[-1]].astype(F32) + adapter.astype(F32)).astype(BF16)

    base_far(nz - 1)
    pl.semaphore_wait(barrier, n - 1 + dp - 1)

    each(0, nz, lambda o: far_copy(o).start())
    each(1, nz, lambda o: near_copy(o).start())
    each(1, n, lambda o: uc_copy(o).start())
    bx_copy(nz - 1).start()
    each(1, dp, lambda o: signal(fence, (d + o) % dp, j))
    for v in range(nz - 2, -1, -1):
        base_far(v)
    for v in range(nz - 1, -1, -1):
        base_own(v)
    for one in loads[2:]:
        one.wait()
    received(dw.at[0:nz - 1, 0:half], wd_r.at[0])
    dw_near.start()
    received(dw.at[0:nz, 0:half, 0:fh], wd_r.at[1])
    dw_y.start()
    dw_far.start()
    received(uc.at[0:n - 1], uc_r.at[0])
    upall = uc[...].reshape(n * rank, chunk)
    pick(sb, lambda at: jnp.dot(upall, cot[:, at], preferred_element_type=F32), SCALE)
    reduce_send(sb, rb, rb_s, rb_r)
    bx_copy(nz - 2).start()
    each(1, n, lambda o: up_copy(o).start())
    for v in range(nz - 3, 0, -1):
        bx_copy(v).start()
    dw_y.wait_recv()
    dw_next.start()
    dw_near.wait_recv()
    dw_far.wait_recv()
    dw_next.wait_recv()
    downall = dw[...].reshape(n * rank, feat)
    pick(sh, lambda at: lax.dot_general(downall, tok[at, :], TRAIL, preferred_element_type=F32), 1.0)
    reduce_send(sh, rh, rh_s, rh_r)
    spread_send(rb, rb_r, ball, ab_s, ab_r)
    bx_copy(0).start()
    advance(1)
    received(uw.at[0:n - 1, 0:half], uw_r.at[0])
    up_mate().start()
    spread_send(rh, rh_r, hall, ah_s, ah_r)
    advance(2)
    but_own(ball, blocks, reduces, received, ab_r.at[0])
    masked(ball)
    gs[0:nz] = grads_of((1 - core) * nz)
    gx_copy.start()
    gs[nz:n] = grads_of(core * nz)
    advance(1)
    pl.semaphore_wait(fence, dp - 1)
    gx_copy.wait_recv()
    each(0, nz // 2, gd_step)
    but_own(hall, blocks, reduces, received, ah_r.at[0])
    masked(hall)
    gu_make()
    each(1, dp * n, lambda o: gu_copy(o).start())
    own_u.start()
    each(nz // 2, nz, gd_step)
    own_start()
    received(uw.at[:, 0:half], um_r.at[0])
    adapt()
    advance(len(steps))
    received(bn.at[starts[-1]], bn_r.at[starts[-1]])
    finish()
    out_copy.start()
    but_own(gr, ny * per, own_gd, received, g_r.at[0])
    received(ur.at[0:dp * n - 1], u_r.at[0])
    own_u.wait()
    out_copy.wait()
    own_wait()

    sent(uc.at[0:n - 1], uc_s.at[0])
    sent(dw.at[0:nz - 1, 0:half], wd_s.at[0])
    sent(dw.at[0:nz, 0:half, 0:fh], wd_s.at[1])
    dw_y.wait_send()
    dw_near.wait_send()
    sent(dw.at[0:nz, 0:half], wm_s.at[1])
    sent(uw.at[0:n - 1, 0:half], uw_s.at[0])
    sent(uw.at[:, 0:half], um_s.at[0])
    but_own(sb, blocks, reduces, sent, rb_s.at[0])
    but_own(sh, blocks, reduces, sent, rh_s.at[0])

    @pl.when(reduces)
    def _():
        sent(rb.at[0:n - 1], ab_s.at[0])
        sent(rh.at[0:n - 1], ah_s.at[0])

    sent(bx, bx_s.at[0])
    sent(bn.at[0:nz - 1], bn_s.at[0])
    gx_copy.wait_send()
    but_own(gs, nz, own_gd, sent, g_s.at[0])
    sent(ur.at[0:dp * n - 1], u_s.at[0])


def tail(dp, per, share, out_in, gr, ur, out, gdown, gup):
    out[...] = out_in[...]
    n = ur.shape[0] // dp
    feat, chunk = gr.shape[2], ur.shape[2]
    for q in range(per):
        gdown[:, q * feat:(q + 1) * feat] = sum(gr[k].astype(F32) for k in range(q, gr.shape[0], per))
    for c in range(n // share):
        gup[:, c * chunk:(c + 1) * chunk] = sum(
            ur[k * n + c * share + i].astype(F32) for k in range(dp) for i in range(share))


def solution(mesh):
    dp, n = mesh.shape["dp"], mesh.shape["tensor"]

    def shards(tokens, cotangent, w, down, up, member):
        rows, feat = tokens.shape
        cw, width, rank = cotangent.shape[1], w.shape[1], up.shape[1]
        per, nz, ny = n // dp, n // 2, dp // 2
        part_rows, blocks = rows // n, rows // BLK
        chunk = max(cw, 128)
        group = blocks if blocks <= 8 else (2 if blocks % 2 == 0 else 1)
        vmem = pl.BlockSpec(memory_space=pltpu.VMEM)
        anywhere = pl.BlockSpec(memory_space=pl.ANY)
        dma = lambda k: pltpu.SemaphoreType.DMA((k,))
        plain = part_rows % 16 == 0
        parts = pl.pallas_call(
            functools.partial(kernel, n, dp),
            out_shape=(
                jax.ShapeDtypeStruct((part_rows, width), BF16),
                jax.ShapeDtypeStruct((ny * per, rank, feat), BF16),
                jax.ShapeDtypeStruct((dp * n, rank // dp, chunk), BF16),
            ),
            in_specs=[pl.BlockSpec(memory_space=pltpu.SMEM)] + [anywhere] * 5,
            out_specs=(anywhere,) * 3,
            scratch_shapes=[
                pltpu.VMEM((rows, feat), BF16),
                pltpu.VMEM((chunk, rows), BF16),
                pltpu.VMEM((feat, width), BF16),
                pltpu.VMEM((n, rank, feat), BF16),
                pltpu.VMEM((n, rank, chunk), BF16),
                pltpu.VMEM((n, rank, width), BF16),
                pltpu.VMEM((n, part_rows, width), BF16),
                pltpu.VMEM((nz, part_rows, width), BF16),
                pltpu.VMEM((nz, part_rows, width), BF16),
                pltpu.VMEM((8, 128) if plain else (rows, width), F32),
                pltpu.VMEM((part_rows, width), BF16),
                pltpu.VMEM((n, rank, group * BLK), F32),
                pltpu.VMEM((blocks, rank, BLK), BF16),
                pltpu.VMEM((n, rank, BLK), BF16),
                pltpu.VMEM((blocks, rank, BLK), BF16),
                pltpu.VMEM((n, rank, BLK), BF16),
                pltpu.VMEM((blocks, rank, BLK), BF16),
                pltpu.VMEM((blocks, rank, BLK), BF16),
                pltpu.VMEM((n * rank, rows), BF16),
                pltpu.VMEM((n, rank, feat), BF16),
                pltpu.VMEM((nz, rank, feat), BF16),
                pltpu.VMEM((2 * BLK, width), F32),
                pltpu.VMEM((dp, n, rank // dp, chunk), BF16),
                dma(6), dma(3),
                dma(1), dma(1), dma(2), dma(2), dma(1), dma(1), dma(2), dma(3), dma(1), dma(1), dma(1), dma(1),
                dma(1), dma(nz), dma(1), dma(nz), *[dma(1) for _ in range(8)],
                pltpu.SemaphoreType.DMA, pltpu.SemaphoreType.DMA, dma(1), dma(1),
                dma(1), dma(1), pltpu.SemaphoreType.REGULAR,
            ],
            compiler_params=pltpu.CompilerParams(
                collective_id=0, has_side_effects=True, vmem_limit_bytes=56 * 1024 * 1024),
        )(member[:, 0], tokens, cotangent.T, w, down[0], up[0])
        out, gdown, gup = pl.pallas_call(
            functools.partial(tail, dp, per, chunk // cw),
            out_shape=(
                jax.ShapeDtypeStruct((part_rows, width), BF16),
                jax.ShapeDtypeStruct((rank, per * feat), F32),
                jax.ShapeDtypeStruct((rank // dp, width), F32),
            ),
            in_specs=[vmem] * 3,
            out_specs=(vmem,) * 3,
        )(*parts)
        return out, gdown[None], gup[None]

    return jax.shard_map(
        shards,
        mesh=mesh,
        in_specs=(P("dp", "tensor"), P("dp", "tensor"), P("tensor", None), P("tensor", None, None),
                  P("tensor", None, None), P("dp", None)),
        out_specs=(P(("dp", "tensor"), None), P("tensor", None, "dp"), P("tensor", "dp", None)),
        check_vma=False,
    )
```

```python
import functools

import jax
import jax.numpy as jnp
from jax import lax
from jax.experimental import pallas as pl
from jax.experimental.pallas import tpu as pltpu
from jax.sharding import PartitionSpec as P

BLK = 128
SCALE = 2.0
TRAIL = (((1,), (1,)), ((), ()))
LEAD = (((0,), (0,)), ((), ()))
F32 = jnp.float32
BF16 = jnp.bfloat16


def levels_of(nz):
    return [1 << l for l in range(nz.bit_length() - 1)]


def each(lo, hi, fn):
    if hi - lo <= 16:
        for k in range(lo, hi):
            fn(k)
    else:
        def step(k, c):
            fn(k)
            return c
        lax.fori_loop(lo, hi, step, 0)


def kernel(n, dp, member, tok_h, cot_h, w_h, down_h, up_h, out_h, gr, ur,
           tok, cot, w, dw, uc, uw, bs, bx, bn, acc, out, sel, sb, rb, sh, rh, ball, hall, gm, gs, gx, gy, blank, ad,
           us, in_s, oc_s, uc_s, uc_r, wd_s, wd_r, wy_s, wy_r, wm_s, wm_r, uw_s, uw_r, um_s, um_r,
           bx_s, bx_r, bn_s, bn_r, rb_s, rb_r, ab_s, ab_r, rh_s, rh_r, ah_s, ah_r, gx_s, gx_r, gy_s, gy_r, g_s, g_r,
           u_s, u_r, fence):
    d = lax.axis_index("dp")
    j = lax.axis_index("tensor")
    rows, feat = tok.shape
    part_rows = rows // n
    rank = dw.shape[1]
    width = w.shape[1]
    chunk = cot.shape[0]
    cw = cot_h.shape[0]
    share = chunk // cw
    half = rank // 2
    ny = dp // 2
    per = n // dp
    nz = n // 2
    blocks = rows // BLK
    core = d % 2
    mate = d + 1 - 2 * core
    ybit = (d // 2) % 2
    ymate = d + 2 - 4 * ybit
    px = j % 2
    zme = j // 2
    partner = j + 1 - 2 * px
    mine = pl.ds(pl.multiple_of(core * half, half), half)
    fh = feat // 2
    cols = pl.ds(pl.multiple_of(ybit * fh, fh), fh)
    ycols = pl.ds(pl.multiple_of((1 - ybit) * fh, fh), fh)
    side = j // nz

    def rcopy(src, dst, s, r, dd, tt):
        return pltpu.make_async_remote_copy(
            src_ref=src, dst_ref=dst, send_sem=s, recv_sem=r,
            device_id={"dp": dd, "tensor": tt}, device_id_type=pl.DeviceIdType.MESH)

    def received(ref, sem):
        rcopy(ref, ref, sem, sem, d, partner).wait_recv()

    def sent(ref, sem):
        rcopy(ref, ref, sem, sem, d, partner).wait_send()

    def peer(o):
        return (j + o) % n

    def block_owner(k):
        return (k * n) // blocks

    my_block = (j * blocks + n - 1) // n
    reduces = jnp.logical_and(my_block < blocks, (my_block * n) // blocks == j)
    block_at = jnp.minimum(my_block, blocks - 1)

    barrier = pltpu.get_barrier_semaphore()

    def signal(sem, dd, tt):
        pl.semaphore_signal(sem, inc=1, device_id={"dp": dd, "tensor": tt}, device_id_type=pl.DeviceIdType.MESH)

    each(1, n, lambda o: signal(barrier, d, peer(o)))
    each(1, dp, lambda o: signal(barrier, (d + o) % dp, j))
    cot[...] = jnp.zeros_like(cot)
    loads = [pltpu.make_async_copy(a, b, in_s.at[k]) for k, (a, b) in enumerate((
        (w_h, w), (tok_h, tok),
        (cot_h, cot.at[pl.ds(pl.multiple_of((j % share) * cw, cw), cw)]),
        (up_h.at[:, pl.ds(pl.multiple_of((j // share) * chunk, chunk), chunk)], uc.at[j]),
        (down_h.at[mine, pl.ds(pl.multiple_of(j * feat, feat), feat)], dw.at[j, mine]),
        (up_h.at[mine], uw.at[j, mine])))]
    for one in loads:
        one.start()
    loads[0].wait()
    loads[1].wait()

    if part_rows % 16 == 0:
        def base(i):
            x = tok[pl.ds(pl.multiple_of(i * part_rows, 16), part_rows), :]
            bs[i] = jnp.dot(x, w[...], preferred_element_type=F32).astype(BF16)
    else:
        def whole(k):
            at = pl.ds(pl.multiple_of(k * BLK, BLK), BLK)
            acc[at, :] = jnp.dot(tok[at, :], w[...], preferred_element_type=F32)

        each(0, blocks, whole)

        def base(i):
            bs[i] = acc[pl.ds(pl.multiple_of(i * part_rows, 8), part_rows), :].astype(BF16)

    masks = levels_of(nz)
    starts = [nz - nz // m for m in masks]

    def bx_copy(v):
        z = zme ^ v
        return rcopy(bs.at[2 * z + 1 - px], bx.at[v], bx_s.at[0], bx_r.at[v], d, partner)

    def base_far(v):
        base(2 * (zme ^ v) + 1 - px)

    def base_own(v):
        base(2 * (zme ^ v) + px)

    def bn_copy(l, c):
        m = masks[l]
        at = starts[l] + c // (2 * m)
        return rcopy(bs.at[2 * (zme ^ m ^ c) + px], bn.at[at], bn_s.at[0], bn_r.at[at], d, 2 * (zme ^ m) + px)

    def bx_step(v):
        received(bx.at[v], bx_r.at[v])
        i = 2 * (zme ^ v) + px
        bs[i] = (bs[i].astype(F32) + bx[v].astype(F32)).astype(BF16)
        if v % 2:
            bn_copy(0, v - 1).start()

    def bn_step(l, c):
        at = starts[l] + c // (2 * masks[l])
        received(bn.at[at], bn_r.at[at])
        i = 2 * (zme ^ c) + px
        bs[i] = (bs[i].astype(F32) + bn[at].astype(F32)).astype(BF16)
        if c & masks[l + 1]:
            bn_copy(l + 1, c - masks[l + 1]).start()

    steps = []
    for v in range(nz - 1, -1, -1):
        steps.append(functools.partial(bx_step, v))
        if v % 2 and v + 1 < nz:
            steps.append(functools.partial(bn_step, 0, v + 1))
    steps.append(functools.partial(bn_step, 0, 0))
    for l in range(1, len(masks) - 1):
        for c in range(nz - 2 * masks[l], -1, -2 * masks[l]):
            steps.append(functools.partial(bn_step, l, c))

    def advance(k):
        for _ in range(min(k, len(steps))):
            steps.pop(0)()

    def uc_copy(o):
        t = peer(o)
        return rcopy(up_h.at[:, pl.ds(pl.multiple_of((t // share) * chunk, chunk), chunk)], uc.at[j],
                     uc_s.at[0], uc_r.at[0], d, t)

    def near_copy(o):
        t = side * nz + (j + o) % nz
        return rcopy(down_h.at[mine, pl.ds(pl.multiple_of(t * feat, feat), feat)], dw.at[j, mine],
                     wd_s.at[0], wd_r.at[0], d, t)

    def far_copy(o):
        t = (1 - side) * nz + (j + o) % nz
        return rcopy(down_h.at[mine, pl.ds(pl.multiple_of(t * feat + ybit * fh, fh), fh)], dw.at[j, mine, cols],
                     wd_s.at[1], wd_r.at[1], d, t)

    near = pl.ds(side * nz, nz)
    distant = pl.ds((1 - side) * nz, nz)

    def dw_copy(slots, at, s_sem, r_sem, to):
        ref = dw.at[slots, mine, at]
        return rcopy(ref, ref, s_sem, r_sem, to, j)

    dw_y = dw_copy(distant, cols, wy_s.at[0], wy_r.at[0], ymate)
    dw_near = dw_copy(near, pl.ds(0, feat), wm_s.at[0], wm_r.at[0], mate)
    dw_far = dw_copy(distant, cols, wm_s.at[1], wm_r.at[1], mate)
    dw_next = dw_copy(distant, ycols, wm_s.at[1], wm_r.at[2], mate)

    wh = width // 2
    ucols = pl.ds(pl.multiple_of(ybit * wh, wh), wh)

    def up_near(o):
        return rcopy(up_h.at[mine], uw.at[j, mine], uw_s.at[0], uw_r.at[0], d, side * nz + (j + o) % nz)

    def up_far(o):
        return rcopy(up_h.at[mine, ucols], uw.at[j, mine, ucols], uw_s.at[1], uw_r.at[1],
                     d, (1 - side) * nz + (j + o) % nz)

    ref = uw.at[distant, mine, ucols]
    up_y = rcopy(ref, ref, wy_s.at[1], wy_r.at[1], ymate, j)
    ref = uw.at[:, mine]
    up_mate = rcopy(ref, ref, um_s.at[0], um_r.at[0], mate, j)

    def reduce_send(send, recv, s_sem, r_sem):
        def start(k):
            @pl.when(block_owner(k) != j)
            def _():
                rcopy(send.at[k], recv.at[j], s_sem.at[0], r_sem.at[0], d, block_owner(k)).start()
        each(0, blocks, start)

        @pl.when(reduces)
        def _():
            recv[j] = send[block_at]

    def but_own(ref, wait, sem):
        @pl.when(reduces)
        def _():
            if blocks > 1:
                wait(ref.at[0:blocks - 1], sem)

        @pl.when(jnp.logical_not(reduces))
        def _():
            wait(ref.at[0:blocks], sem)

    def spread_copy(full, s_sem, r_sem, o):
        return rcopy(full.at[block_at], full.at[block_at], s_sem.at[0], r_sem.at[0], d, peer(o))

    def spread_send(recv, r_sem, full, s_sem, f_sem):
        @pl.when(reduces)
        def _():
            received(recv.at[0:n - 1], r_sem.at[0])
            full[block_at] = sum(recv[s].astype(F32) for s in range(n)).astype(BF16)
            each(1, n, lambda o: spread_copy(full, s_sem, f_sem, o).start())

    group = blocks if blocks <= 8 else (2 if blocks % 2 == 0 else 1)

    def pick(dest, make, scale):
        def step(g):
            at = pl.ds(pl.multiple_of(g * group * BLK, BLK), group * BLK)
            sel[...] = (scale * make(at)).reshape(n, rank, group * BLK)
            for i in range(group):
                k = g * group + i
                dest[k] = sel[member[k], :, i * BLK:(i + 1) * BLK].astype(BF16)
        each(0, blocks // group, step)

    def masked(full):
        owner_row = lax.broadcasted_iota(jnp.int32, (n * rank, BLK), 0) // rank
        for k in range(blocks):
            tiled = jnp.concatenate([full[k]] * n, axis=0)
            gm[:, k * BLK:(k + 1) * BLK] = jnp.where(owner_row == member[k], tiled, jnp.zeros_like(tiled))

    def grads_of(lo):
        part = gm[pl.ds(pl.multiple_of(lo * rank, nz * rank), nz * rank), :]
        g = jnp.dot(part, tok[...], preferred_element_type=F32)
        return g.astype(BF16).reshape(nz, rank, feat)

    gx_copy = rcopy(gs.at[0:nz], gx, gx_s, gx_r, mate, j)
    hz = nz // 2
    hq = hz // 2
    first = hz + ybit * hq
    gy_copy = rcopy(gs.at[pl.ds(nz + hz + (1 - ybit) * hq, hq)], gy, gy_s, gy_r, ymate, j)
    dd, row = j // per, (j % per) * ny
    kk = j % nz
    direct = kk < hz
    slot = row + jnp.where(direct, d // 2, d // 4)
    own_gd = jnp.logical_and(jnp.logical_and(dd == d, j // nz == core),
                             jnp.logical_or(direct, jnp.logical_and(kk >= first, kk < first + hq)))

    def gx_add(lo, count):
        at = pl.ds(nz + lo, count)
        gs[at] = (gs[at].astype(F32) + gx[pl.ds(lo, count)].astype(F32)).astype(BF16)

    def gd_send(k, at):
        @pl.when(jnp.logical_or(dd != d, core * nz + k != j))
        def _():
            rcopy(gs.at[nz + k], gr.at[at], g_s.at[0], g_r.at[0], dd, core * nz + k).start()

    def gd_direct(k):
        gx_add(k, 1)
        gd_send(k, row + d // 2)

    def gd_step(k):
        at = nz + first + k
        gs[at] = (gs[at].astype(F32) + gy[k].astype(F32)).astype(BF16)
        gd_send(first + k, row + d // 4)

    def gd_all(ref, when, count, wait, sem):
        @pl.when(jnp.logical_and(when, own_gd))
        def _():
            if count > 1:
                wait(ref.at[0:count - 1], sem)

        @pl.when(jnp.logical_and(when, jnp.logical_not(own_gd)))
        def _():
            wait(ref.at[0:count], sem)

    def blank_copy(q):
        return pltpu.make_async_copy(blank, gr.at[pl.ds(q * ny + ny // 2, ny // 2)], oc_s.at[3 + q])

    def blank_each(act):
        @pl.when(jnp.logical_not(direct))
        def _():
            for q in range(per):
                act(blank_copy(q))

    def own_copy():
        return pltpu.make_async_copy(gs.at[nz + j % nz], gr.at[slot], oc_s.at[0])

    def own_start():
        @pl.when(own_gd)
        def _():
            own_copy().start()

    def own_wait():
        @pl.when(own_gd)
        def _():
            own_copy().wait()

    part = rank // dp

    def gu_make():
        gu = SCALE * lax.dot_general(gm[...], cot[...], TRAIL, preferred_element_type=F32)
        gu = gu.reshape(n, rank, chunk)
        for k in range(dp):
            us[k] = gu[:, k * part:(k + 1) * part, :].astype(us.dtype)

    here = d * n + j

    def gu_copy(o):
        e = (here + o) % (dp * n)
        return rcopy(us.at[e // n, e % n], ur.at[here], u_s.at[0], u_r.at[0], e // n, e % n)

    own_u = pltpu.make_async_copy(us.at[d, j], ur.at[here], oc_s.at[1])
    out_copy = pltpu.make_async_copy(out, out_h, oc_s.at[2])
    k0 = (j * part_rows) // BLK
    k1 = (j * part_rows + part_rows - 1) // BLK

    def adapt():
        ad[0:BLK] = lax.dot_general(hall[k0], uw[member[k0]], LEAD, preferred_element_type=F32)
        ad[BLK:2 * BLK] = lax.dot_general(hall[k1], uw[member[k1]], LEAD, preferred_element_type=F32)

    def finish():
        adapter = (SCALE * ad[pl.ds(pl.multiple_of(j * part_rows - k0 * BLK, 8), part_rows), :]).astype(BF16)
        out[...] = (bs[j].astype(F32) + bn[starts[-1]].astype(F32) + adapter.astype(F32)).astype(BF16)

    base_far(nz - 1)
    pl.semaphore_wait(barrier, n - 1 + dp - 1)

    each(0, nz, lambda o: far_copy(o).start())
    each(1, nz, lambda o: near_copy(o).start())
    each(1, n, lambda o: uc_copy(o).start())
    each(0, nz, lambda o: up_far(o).start())
    each(1, nz, lambda o: up_near(o).start())
    bx_copy(nz - 1).start()
    each(1, dp, lambda o: signal(fence, (d + o) % dp, j))
    for v in range(nz - 2, -1, -1):
        base_far(v)
    for v in range(nz - 1, -1, -1):
        base_own(v)
    blank[...] = jnp.zeros_like(blank)
    blank_each(lambda c: c.start())
    for one in loads[2:]:
        one.wait()
    received(dw.at[0:nz - 1, 0:half], wd_r.at[0])
    dw_near.start()
    received(dw.at[0:nz, 0:half, 0:fh], wd_r.at[1])
    dw_y.start()
    dw_far.start()
    received(uc.at[0:n - 1], uc_r.at[0])
    upall = uc[...].reshape(n * rank, chunk)
    pick(sb, lambda at: jnp.dot(upall, cot[:, at], preferred_element_type=F32), SCALE)
    reduce_send(sb, rb, rb_s, rb_r)
    bx_copy(nz - 2).start()
    advance(1)
    for v in range(nz - 3, 0, -1):
        bx_copy(v).start()
    dw_y.wait_recv()
    dw_next.start()
    dw_near.wait_recv()
    dw_far.wait_recv()
    dw_next.wait_recv()
    downall = dw[...].reshape(n * rank, feat)
    pick(sh, lambda at: lax.dot_general(downall, tok[at, :], TRAIL, preferred_element_type=F32), 1.0)
    reduce_send(sh, rh, rh_s, rh_r)
    spread_send(rb, rb_r, ball, ab_s, ab_r)
    bx_copy(0).start()
    advance(1)
    spread_send(rh, rh_r, hall, ah_s, ah_r)
    advance(2)
    but_own(ball, received, ab_r.at[0])
    masked(ball)
    gs[0:nz] = grads_of((1 - core) * nz)
    gx_copy.start()
    gs[nz:n] = grads_of(core * nz)
    gx_copy.wait_recv()
    gx_add(hz + (1 - ybit) * hq, hq)
    gy_copy.start()
    pl.semaphore_wait(fence, dp - 1)
    each(0, hz, gd_direct)
    gx_add(first, hq)
    but_own(hall, received, ah_r.at[0])
    masked(hall)
    gu_make()
    each(1, dp * n, lambda o: gu_copy(o).start())
    own_u.start()
    gy_copy.wait_recv()
    each(0, hq, gd_step)
    own_start()
    received(uw.at[0:nz, 0:half, 0:wh], uw_r.at[1])
    up_y.start()
    received(uw.at[0:nz - 1, 0:half], uw_r.at[0])
    advance(len(steps))
    up_y.wait_recv()
    up_mate.start()
    received(uw.at[:, 0:half], um_r.at[0])
    adapt()
    received(bn.at[starts[-1]], bn_r.at[starts[-1]])
    finish()
    out_copy.start()
    gd_all(gr, direct, ny * per, received, g_r.at[0])
    gd_all(gr, jnp.logical_not(direct), (ny // 2) * per, received, g_r.at[0])
    blank_each(lambda c: c.wait())
    received(ur.at[0:dp * n - 1], u_r.at[0])
    own_u.wait()
    out_copy.wait()
    own_wait()

    sent(uc.at[0:n - 1], uc_s.at[0])
    sent(dw.at[0:nz - 1, 0:half], wd_s.at[0])
    sent(dw.at[0:nz, 0:half, 0:fh], wd_s.at[1])
    dw_y.wait_send()
    dw_near.wait_send()
    sent(dw.at[0:nz, 0:half], wm_s.at[1])
    sent(uw.at[0:nz - 1, 0:half], uw_s.at[0])
    sent(uw.at[0:nz, 0:half, 0:wh], uw_s.at[1])
    up_y.wait_send()
    up_mate.wait_send()
    but_own(sb, sent, rb_s.at[0])
    but_own(sh, sent, rh_s.at[0])

    @pl.when(reduces)
    def _():
        sent(rb.at[0:n - 1], ab_s.at[0])
        sent(rh.at[0:n - 1], ah_s.at[0])

    sent(bx, bx_s.at[0])
    sent(bn.at[0:nz - 1], bn_s.at[0])
    gx_copy.wait_send()
    gy_copy.wait_send()
    gd_all(gs, True, hz + hq, sent, g_s.at[0])
    sent(ur.at[0:dp * n - 1], u_s.at[0])


def tail(dp, per, share, out_in, gr, ur, out, gdown, gup):
    out[...] = out_in[...]
    n = ur.shape[0] // dp
    feat, chunk = gr.shape[2], ur.shape[2]
    count = gr.shape[0] // per
    for q in range(per):
        gdown[:, q * feat:(q + 1) * feat] = sum(gr[q * count + k].astype(F32) for k in range(count))
    for c in range(n // share):
        gup[:, c * chunk:(c + 1) * chunk] = sum(
            ur[k * n + c * share + i].astype(F32) for k in range(dp) for i in range(share))


def solution(mesh):
    dp, n = mesh.shape["dp"], mesh.shape["tensor"]

    def shards(tokens, cotangent, w, down, up, member):
        rows, feat = tokens.shape
        cw, width, rank = cotangent.shape[1], w.shape[1], up.shape[1]
        per, nz, ny = n // dp, n // 2, dp // 2
        part_rows, blocks = rows // n, rows // BLK
        chunk = max(cw, 128)
        group = blocks if blocks <= 8 else (2 if blocks % 2 == 0 else 1)
        vmem = pl.BlockSpec(memory_space=pltpu.VMEM)
        anywhere = pl.BlockSpec(memory_space=pl.ANY)
        dma = lambda k: pltpu.SemaphoreType.DMA((k,))
        plain = part_rows % 16 == 0
        parts = pl.pallas_call(
            functools.partial(kernel, n, dp),
            out_shape=(
                jax.ShapeDtypeStruct((part_rows, width), BF16),
                jax.ShapeDtypeStruct((ny * per, rank, feat), BF16),
                jax.ShapeDtypeStruct((dp * n, rank // dp, chunk), BF16),
            ),
            in_specs=[pl.BlockSpec(memory_space=pltpu.SMEM)] + [anywhere] * 5,
            out_specs=(anywhere,) * 3,
            scratch_shapes=[
                pltpu.VMEM((rows, feat), BF16),
                pltpu.VMEM((chunk, rows), BF16),
                pltpu.VMEM((feat, width), BF16),
                pltpu.VMEM((n, rank, feat), BF16),
                pltpu.VMEM((n, rank, chunk), BF16),
                pltpu.VMEM((n, rank, width), BF16),
                pltpu.VMEM((n, part_rows, width), BF16),
                pltpu.VMEM((nz, part_rows, width), BF16),
                pltpu.VMEM((nz, part_rows, width), BF16),
                pltpu.VMEM((8, 128) if plain else (rows, width), F32),
                pltpu.VMEM((part_rows, width), BF16),
                pltpu.VMEM((n, rank, group * BLK), F32),
                pltpu.VMEM((blocks, rank, BLK), BF16),
                pltpu.VMEM((n, rank, BLK), BF16),
                pltpu.VMEM((blocks, rank, BLK), BF16),
                pltpu.VMEM((n, rank, BLK), BF16),
                pltpu.VMEM((blocks, rank, BLK), BF16),
                pltpu.VMEM((blocks, rank, BLK), BF16),
                pltpu.VMEM((n * rank, rows), BF16),
                pltpu.VMEM((n, rank, feat), BF16),
                pltpu.VMEM((nz, rank, feat), BF16),
                pltpu.VMEM((nz // 4, rank, feat), BF16),
                pltpu.VMEM((ny // 2, rank, feat), BF16),
                pltpu.VMEM((2 * BLK, width), F32),
                pltpu.VMEM((dp, n, rank // dp, chunk), BF16),
                dma(6), dma(3 + per),
                dma(1), dma(1), dma(2), dma(2), dma(2), dma(2), dma(2), dma(3), dma(2), dma(2), dma(1), dma(1),
                dma(1), dma(nz), dma(1), dma(nz - 1), *[dma(1) for _ in range(8)],
                *[pltpu.SemaphoreType.DMA] * 4, dma(1), dma(1),
                dma(1), dma(1), pltpu.SemaphoreType.REGULAR,
            ],
            compiler_params=pltpu.CompilerParams(
                collective_id=0, has_side_effects=True, vmem_limit_bytes=56 * 1024 * 1024),
        )(member[:, 0], tokens, cotangent.T, w, down[0], up[0])
        out, gdown, gup = pl.pallas_call(
            functools.partial(tail, dp, per, chunk // cw),
            out_shape=(
                jax.ShapeDtypeStruct((part_rows, width), BF16),
                jax.ShapeDtypeStruct((rank, per * feat), F32),
                jax.ShapeDtypeStruct((rank // dp, width), F32),
            ),
            in_specs=[vmem] * 3,
            out_specs=(vmem,) * 3,
        )(*parts)
        return out, gdown[None], gup[None]

    return jax.shard_map(
        shards,
        mesh=mesh,
        in_specs=(P("dp", "tensor"), P("dp", "tensor"), P("tensor", None), P("tensor", None, None),
                  P("tensor", None, None), P("dp", None)),
        out_specs=(P(("dp", "tensor"), None), P("tensor", None, "dp"), P("tensor", "dp", None)),
        check_vma=False,
    )
```

```python
import functools

import jax
import jax.numpy as jnp
from jax import lax
from jax.experimental import pallas as pl
from jax.experimental.pallas import tpu as pltpu
from jax.sharding import PartitionSpec as P

BLK = 128
SCALE = 2.0
TRAIL = (((1,), (1,)), ((), ()))
LEAD = (((0,), (0,)), ((), ()))
F32 = jnp.float32
BF16 = jnp.bfloat16


def levels_of(nz):
    return [1 << l for l in range(nz.bit_length() - 1)]


def each(lo, hi, fn):
    if hi - lo <= 16:
        for k in range(lo, hi):
            fn(k)
    else:
        def step(k, c):
            fn(k)
            return c
        lax.fori_loop(lo, hi, step, 0)


def kernel(n, dp, member, tok_h, cot_h, w_h, down_h, up_h, out_h, gr, ur,
           tok, cot, w, dw, uc, uw, bs, bx, bn, acc, sel, sb, rb, sh, rh, ball, hall, gm, gs, gx, gy, blank, ad,
           us, in_s, oc_s, uc_s, uc_r, wd_s, wd_r, wy_s, wy_r, wm_s, wm_r, uw_s, uw_r, um_s, um_r,
           bx_s, bx_r, bn_s, bn_r, rb_s, rb_r, ab_s, ab_r, rh_s, rh_r, ah_s, ah_r, gx_s, gx_r, gy_s, gy_r, g_s, g_r,
           u_s, u_r, fence):
    d = lax.axis_index("dp")
    j = lax.axis_index("tensor")
    rows, feat = tok.shape
    part_rows = rows // n
    rank = dw.shape[1]
    width = w.shape[1]
    chunk = cot.shape[0]
    cw = cot_h.shape[0]
    share = chunk // cw
    half = rank // 2
    ny = dp // 2
    per = n // dp
    nz = n // 2
    blocks = rows // BLK
    core = d % 2
    mate = d + 1 - 2 * core
    ybit = (d // 2) % 2
    ymate = d + 2 - 4 * ybit
    px = j % 2
    zme = j // 2
    partner = j + 1 - 2 * px
    mine = pl.ds(pl.multiple_of(core * half, half), half)
    fh = feat // 2
    cols = pl.ds(pl.multiple_of(ybit * fh, fh), fh)
    ycols = pl.ds(pl.multiple_of((1 - ybit) * fh, fh), fh)
    side = j // nz

    def rcopy(src, dst, s, r, dd, tt):
        return pltpu.make_async_remote_copy(
            src_ref=src, dst_ref=dst, send_sem=s, recv_sem=r,
            device_id={"dp": dd, "tensor": tt}, device_id_type=pl.DeviceIdType.MESH)

    def received(ref, sem):
        rcopy(ref, ref, sem, sem, d, partner).wait_recv()

    def sent(ref, sem):
        rcopy(ref, ref, sem, sem, d, partner).wait_send()

    def peer(o):
        return (j + o) % n

    def block_owner(k):
        return (k * n) // blocks

    my_block = (j * blocks + n - 1) // n
    reduces = jnp.logical_and(my_block < blocks, (my_block * n) // blocks == j)
    block_at = jnp.minimum(my_block, blocks - 1)

    barrier = pltpu.get_barrier_semaphore()

    def signal(sem, dd, tt):
        pl.semaphore_signal(sem, inc=1, device_id={"dp": dd, "tensor": tt}, device_id_type=pl.DeviceIdType.MESH)

    each(1, n, lambda o: signal(barrier, d, peer(o)))
    each(1, dp, lambda o: signal(barrier, (d + o) % dp, j))
    cot[...] = jnp.zeros_like(cot)
    loads = [pltpu.make_async_copy(a, b, in_s.at[k]) for k, (a, b) in enumerate((
        (w_h, w), (tok_h, tok),
        (cot_h, cot.at[pl.ds(pl.multiple_of((j % share) * cw, cw), cw)]),
        (up_h.at[:, pl.ds(pl.multiple_of((j // share) * chunk, chunk), chunk)], uc.at[j]),
        (down_h.at[mine, pl.ds(pl.multiple_of(j * feat, feat), feat)], dw.at[j, mine]),
        (up_h.at[mine], uw.at[j, mine])))]
    for one in loads:
        one.start()
    loads[0].wait()
    loads[1].wait()

    if part_rows % 16 == 0:
        def base(i):
            x = tok[pl.ds(pl.multiple_of(i * part_rows, 16), part_rows), :]
            bs[i] = jnp.dot(x, w[...], preferred_element_type=F32).astype(BF16)
    else:
        def whole(k):
            at = pl.ds(pl.multiple_of(k * BLK, BLK), BLK)
            acc[at, :] = jnp.dot(tok[at, :], w[...], preferred_element_type=F32)

        each(0, blocks, whole)

        def base(i):
            bs[i] = acc[pl.ds(pl.multiple_of(i * part_rows, 8), part_rows), :].astype(BF16)

    masks = levels_of(nz)
    starts = [nz - nz // m for m in masks]

    def bx_copy(v):
        z = zme ^ v
        return rcopy(bs.at[2 * z + 1 - px], bx.at[v], bx_s.at[0], bx_r.at[v], d, partner)

    def base_far(v):
        base(2 * (zme ^ v) + 1 - px)

    def base_own(v):
        base(2 * (zme ^ v) + px)

    def bn_copy(l, c):
        m = masks[l]
        at = starts[l] + c // (2 * m)
        return rcopy(bs.at[2 * (zme ^ m ^ c) + px], bn.at[at], bn_s.at[0], bn_r.at[at], d, 2 * (zme ^ m) + px)

    def bx_step(v):
        received(bx.at[v], bx_r.at[v])
        i = 2 * (zme ^ v) + px
        bs[i] = (bs[i].astype(F32) + bx[v].astype(F32)).astype(BF16)
        if v % 2:
            bn_copy(0, v - 1).start()

    def bn_step(l, c):
        at = starts[l] + c // (2 * masks[l])
        received(bn.at[at], bn_r.at[at])
        i = 2 * (zme ^ c) + px
        bs[i] = (bs[i].astype(F32) + bn[at].astype(F32)).astype(BF16)
        if c & masks[l + 1]:
            bn_copy(l + 1, c - masks[l + 1]).start()

    steps = []
    for v in range(nz - 1, -1, -1):
        steps.append(functools.partial(bx_step, v))
        if v % 2 and v + 1 < nz:
            steps.append(functools.partial(bn_step, 0, v + 1))
    steps.append(functools.partial(bn_step, 0, 0))
    for l in range(1, len(masks) - 1):
        for c in range(nz - 2 * masks[l], -1, -2 * masks[l]):
            steps.append(functools.partial(bn_step, l, c))

    def advance(k):
        for _ in range(min(k, len(steps))):
            steps.pop(0)()

    def uc_copy(o):
        t = peer(o)
        return rcopy(up_h.at[:, pl.ds(pl.multiple_of((t // share) * chunk, chunk), chunk)], uc.at[j],
                     uc_s.at[0], uc_r.at[0], d, t)

    def near_copy(o):
        t = side * nz + (j + o) % nz
        return rcopy(down_h.at[mine, pl.ds(pl.multiple_of(t * feat, feat), feat)], dw.at[j, mine],
                     wd_s.at[0], wd_r.at[0], d, t)

    def far_copy(o):
        t = (1 - side) * nz + (j + o) % nz
        return rcopy(down_h.at[mine, pl.ds(pl.multiple_of(t * feat + ybit * fh, fh), fh)], dw.at[j, mine, cols],
                     wd_s.at[1], wd_r.at[1], d, t)

    near = pl.ds(side * nz, nz)
    distant = pl.ds((1 - side) * nz, nz)

    def dw_copy(slots, at, s_sem, r_sem, to):
        ref = dw.at[slots, mine, at]
        return rcopy(ref, ref, s_sem, r_sem, to, j)

    dw_y = dw_copy(distant, cols, wy_s.at[0], wy_r.at[0], ymate)
    dw_near = dw_copy(near, pl.ds(0, feat), wm_s.at[0], wm_r.at[0], mate)
    dw_far = dw_copy(distant, cols, wm_s.at[1], wm_r.at[1], mate)
    dw_next = dw_copy(distant, ycols, wm_s.at[1], wm_r.at[2], mate)

    wh = width // 2
    ucols = pl.ds(pl.multiple_of(ybit * wh, wh), wh)

    def up_near(o):
        return rcopy(up_h.at[mine], uw.at[j, mine], uw_s.at[0], uw_r.at[0], d, side * nz + (j + o) % nz)

    def up_far(o):
        return rcopy(up_h.at[mine, ucols], uw.at[j, mine, ucols], uw_s.at[1], uw_r.at[1],
                     d, (1 - side) * nz + (j + o) % nz)

    ref = uw.at[distant, mine, ucols]
    up_y = rcopy(ref, ref, wy_s.at[1], wy_r.at[1], ymate, j)
    ref = uw.at[:, mine]
    up_mate = rcopy(ref, ref, um_s.at[0], um_r.at[0], mate, j)

    def reduce_send(send, recv, s_sem, r_sem):
        def start(k):
            @pl.when(block_owner(k) != j)
            def _():
                rcopy(send.at[k], recv.at[j], s_sem.at[0], r_sem.at[0], d, block_owner(k)).start()
        each(0, blocks, start)

        @pl.when(reduces)
        def _():
            recv[j] = send[block_at]

    def but_own(ref, wait, sem):
        @pl.when(reduces)
        def _():
            if blocks > 1:
                wait(ref.at[0:blocks - 1], sem)

        @pl.when(jnp.logical_not(reduces))
        def _():
            wait(ref.at[0:blocks], sem)

    def spread_copy(full, s_sem, r_sem, o):
        return rcopy(full.at[block_at], full.at[block_at], s_sem.at[0], r_sem.at[0], d, peer(o))

    def spread_send(recv, r_sem, full, s_sem, f_sem):
        @pl.when(reduces)
        def _():
            received(recv.at[0:n - 1], r_sem.at[0])
            full[block_at] = sum(recv[s].astype(F32) for s in range(n)).astype(BF16)
            each(1, n, lambda o: spread_copy(full, s_sem, f_sem, o).start())

    group = blocks if blocks <= 8 else (2 if blocks % 2 == 0 else 1)

    def pick(dest, make, scale):
        def step(g):
            at = pl.ds(pl.multiple_of(g * group * BLK, BLK), group * BLK)
            sel[...] = (scale * make(at)).reshape(n, rank, group * BLK)
            for i in range(group):
                k = g * group + i
                dest[k] = sel[member[k], :, i * BLK:(i + 1) * BLK].astype(BF16)
        each(0, blocks // group, step)

    def masked(full):
        owner_row = lax.broadcasted_iota(jnp.int32, (n * rank, BLK), 0) // rank
        for k in range(blocks):
            tiled = jnp.concatenate([full[k]] * n, axis=0)
            gm[:, k * BLK:(k + 1) * BLK] = jnp.where(owner_row == member[k], tiled, jnp.zeros_like(tiled))

    def grads_of(lo):
        part = gm[pl.ds(pl.multiple_of(lo * rank, nz * rank), nz * rank), :]
        g = jnp.dot(part, tok[...], preferred_element_type=F32)
        return g.astype(BF16).reshape(nz, rank, feat)

    gx_copy = rcopy(gs.at[0:nz], gx, gx_s, gx_r, mate, j)
    hz = nz // 2
    hq = hz // 2
    first = hz + ybit * hq
    gy_copy = rcopy(gs.at[pl.ds(nz + hz + (1 - ybit) * hq, hq)], gy, gy_s, gy_r, ymate, j)
    dd, row = j // per, (j % per) * ny
    kk = j % nz
    direct = kk < hz
    slot = row + jnp.where(direct, d // 2, d // 4)
    own_gd = jnp.logical_and(jnp.logical_and(dd == d, j // nz == core),
                             jnp.logical_or(direct, jnp.logical_and(kk >= first, kk < first + hq)))

    def gx_add(lo, count):
        at = pl.ds(nz + lo, count)
        gs[at] = (gs[at].astype(F32) + gx[pl.ds(lo, count)].astype(F32)).astype(BF16)

    def gd_send(k, at):
        @pl.when(jnp.logical_or(dd != d, core * nz + k != j))
        def _():
            rcopy(gs.at[nz + k], gr.at[at], g_s.at[0], g_r.at[0], dd, core * nz + k).start()

    def gd_direct(k):
        gx_add(k, 1)
        gd_send(k, row + d // 2)

    def gd_step(k):
        at = nz + first + k
        gs[at] = (gs[at].astype(F32) + gy[k].astype(F32)).astype(BF16)
        gd_send(first + k, row + d // 4)

    def gd_all(ref, when, count, wait, sem):
        @pl.when(jnp.logical_and(when, own_gd))
        def _():
            if count > 1:
                wait(ref.at[0:count - 1], sem)

        @pl.when(jnp.logical_and(when, jnp.logical_not(own_gd)))
        def _():
            wait(ref.at[0:count], sem)

    def blank_copy(q):
        return pltpu.make_async_copy(blank, gr.at[pl.ds(q * ny + ny // 2, ny // 2)], oc_s.at[3 + q])

    def blank_each(act):
        @pl.when(jnp.logical_not(direct))
        def _():
            for q in range(per):
                act(blank_copy(q))

    def own_copy():
        return pltpu.make_async_copy(gs.at[nz + j % nz], gr.at[slot], oc_s.at[0])

    def own_start():
        @pl.when(own_gd)
        def _():
            own_copy().start()

    def own_wait():
        @pl.when(own_gd)
        def _():
            own_copy().wait()

    part = rank // dp

    def gu_make():
        gu = SCALE * lax.dot_general(gm[...], cot[...], TRAIL, preferred_element_type=F32)
        gu = gu.reshape(n, rank, chunk)
        for k in range(dp):
            us[k] = gu[:, k * part:(k + 1) * part, :].astype(us.dtype)

    here = d * n + j

    def gu_copy(o):
        e = (here + o) % (dp * n)
        return rcopy(us.at[e // n, e % n], ur.at[here], u_s.at[0], u_r.at[0], e // n, e % n)

    own_u = pltpu.make_async_copy(us.at[d, j], ur.at[here], oc_s.at[1])
    k0 = (j * part_rows) // BLK
    k1 = (j * part_rows + part_rows - 1) // BLK

    def adapt():
        ad[0:BLK] = lax.dot_general(hall[k0], uw[member[k0]], LEAD, preferred_element_type=F32)
        ad[BLK:2 * BLK] = lax.dot_general(hall[k1], uw[member[k1]], LEAD, preferred_element_type=F32)

    def finish():
        adapter = (SCALE * ad[pl.ds(pl.multiple_of(j * part_rows - k0 * BLK, 8), part_rows), :]).astype(BF16)
        out_h[...] = (bs[j].astype(F32) + bn[starts[-1]].astype(F32) + adapter.astype(F32)).astype(BF16)

    base_far(nz - 1)
    pl.semaphore_wait(barrier, n - 1 + dp - 1)

    each(0, nz, lambda o: far_copy(o).start())
    each(1, nz, lambda o: near_copy(o).start())
    each(1, n, lambda o: uc_copy(o).start())
    each(0, nz, lambda o: up_far(o).start())
    each(1, nz, lambda o: up_near(o).start())
    bx_copy(nz - 1).start()
    each(1, dp, lambda o: signal(fence, (d + o) % dp, j))
    for v in range(nz - 2, -1, -1):
        base_far(v)
    for v in range(nz - 1, -1, -1):
        base_own(v)
    blank[...] = jnp.zeros_like(blank)
    blank_each(lambda c: c.start())
    for one in loads[2:]:
        one.wait()
    received(dw.at[0:nz - 1, 0:half], wd_r.at[0])
    dw_near.start()
    received(dw.at[0:nz, 0:half, 0:fh], wd_r.at[1])
    dw_y.start()
    dw_far.start()
    received(uc.at[0:n - 1], uc_r.at[0])
    upall = uc[...].reshape(n * rank, chunk)
    pick(sb, lambda at: jnp.dot(upall, cot[:, at], preferred_element_type=F32), SCALE)
    reduce_send(sb, rb, rb_s, rb_r)
    bx_copy(nz - 2).start()
    advance(1)
    for v in range(nz - 3, 0, -1):
        bx_copy(v).start()
    dw_y.wait_recv()
    dw_next.start()
    dw_near.wait_recv()
    dw_far.wait_recv()
    dw_next.wait_recv()
    downall = dw[...].reshape(n * rank, feat)
    pick(sh, lambda at: lax.dot_general(downall, tok[at, :], TRAIL, preferred_element_type=F32), 1.0)
    reduce_send(sh, rh, rh_s, rh_r)
    spread_send(rb, rb_r, ball, ab_s, ab_r)
    bx_copy(0).start()
    advance(1)
    spread_send(rh, rh_r, hall, ah_s, ah_r)
    advance(2)
    but_own(ball, received, ab_r.at[0])
    masked(ball)
    gs[0:nz] = grads_of((1 - core) * nz)
    gx_copy.start()
    gs[nz:n] = grads_of(core * nz)
    gx_copy.wait_recv()
    gx_add(hz + (1 - ybit) * hq, hq)
    gy_copy.start()
    pl.semaphore_wait(fence, dp - 1)
    each(0, hz, gd_direct)
    gx_add(first, hq)
    but_own(hall, received, ah_r.at[0])
    masked(hall)
    gu_make()
    each(1, dp * n, lambda o: gu_copy(o).start())
    own_u.start()
    gy_copy.wait_recv()
    each(0, hq, gd_step)
    own_start()
    received(uw.at[0:nz, 0:half, 0:wh], uw_r.at[1])
    up_y.start()
    received(uw.at[0:nz - 1, 0:half], uw_r.at[0])
    advance(len(steps))
    up_y.wait_recv()
    up_mate.start()
    received(uw.at[:, 0:half], um_r.at[0])
    adapt()
    received(bn.at[starts[-1]], bn_r.at[starts[-1]])
    finish()
    gd_all(gr, direct, ny * per, received, g_r.at[0])
    gd_all(gr, jnp.logical_not(direct), (ny // 2) * per, received, g_r.at[0])
    blank_each(lambda c: c.wait())
    received(ur.at[0:dp * n - 1], u_r.at[0])
    own_u.wait()
    own_wait()

    sent(uc.at[0:n - 1], uc_s.at[0])
    sent(dw.at[0:nz - 1, 0:half], wd_s.at[0])
    sent(dw.at[0:nz, 0:half, 0:fh], wd_s.at[1])
    dw_y.wait_send()
    dw_near.wait_send()
    sent(dw.at[0:nz, 0:half], wm_s.at[1])
    sent(uw.at[0:nz - 1, 0:half], uw_s.at[0])
    sent(uw.at[0:nz, 0:half, 0:wh], uw_s.at[1])
    up_y.wait_send()
    up_mate.wait_send()
    but_own(sb, sent, rb_s.at[0])
    but_own(sh, sent, rh_s.at[0])

    @pl.when(reduces)
    def _():
        sent(rb.at[0:n - 1], ab_s.at[0])
        sent(rh.at[0:n - 1], ah_s.at[0])

    sent(bx, bx_s.at[0])
    sent(bn.at[0:nz - 1], bn_s.at[0])
    gx_copy.wait_send()
    gy_copy.wait_send()
    gd_all(gs, True, hz + hq, sent, g_s.at[0])
    sent(ur.at[0:dp * n - 1], u_s.at[0])


def tail(dp, per, share, out_in, gr, ur, out, gdown, gup):
    out[...] = out_in[...]
    n = ur.shape[0] // dp
    feat, chunk = gr.shape[2], ur.shape[2]
    count = gr.shape[0] // per
    for q in range(per):
        gdown[:, q * feat:(q + 1) * feat] = sum(gr[q * count + k].astype(F32) for k in range(count))
    for c in range(n // share):
        gup[:, c * chunk:(c + 1) * chunk] = sum(
            ur[k * n + c * share + i].astype(F32) for k in range(dp) for i in range(share))


def solution(mesh):
    dp, n = mesh.shape["dp"], mesh.shape["tensor"]

    def shards(tokens, cotangent, w, down, up, member):
        rows, feat = tokens.shape
        cw, width, rank = cotangent.shape[1], w.shape[1], up.shape[1]
        per, nz, ny = n // dp, n // 2, dp // 2
        part_rows, blocks = rows // n, rows // BLK
        chunk = max(cw, 128)
        group = blocks if blocks <= 8 else (2 if blocks % 2 == 0 else 1)
        vmem = pl.BlockSpec(memory_space=pltpu.VMEM)
        anywhere = pl.BlockSpec(memory_space=pl.ANY)
        dma = lambda k: pltpu.SemaphoreType.DMA((k,))
        plain = part_rows % 16 == 0
        parts = pl.pallas_call(
            functools.partial(kernel, n, dp),
            out_shape=(
                pltpu.VMEM((part_rows, width), BF16),
                pltpu.VMEM((ny * per, rank, feat), BF16),
                pltpu.VMEM((dp * n, rank // dp, chunk), BF16),
            ),
            in_specs=[pl.BlockSpec(memory_space=pltpu.SMEM)] + [anywhere] * 5,
            out_specs=(vmem,) * 3,
            scratch_shapes=[
                pltpu.VMEM((rows, feat), BF16),
                pltpu.VMEM((chunk, rows), BF16),
                pltpu.VMEM((feat, width), BF16),
                pltpu.VMEM((n, rank, feat), BF16),
                pltpu.VMEM((n, rank, chunk), BF16),
                pltpu.VMEM((n, rank, width), BF16),
                pltpu.VMEM((n, part_rows, width), BF16),
                pltpu.VMEM((nz, part_rows, width), BF16),
                pltpu.VMEM((nz, part_rows, width), BF16),
                pltpu.VMEM((8, 128) if plain else (rows, width), F32),
                pltpu.VMEM((n, rank, group * BLK), F32),
                pltpu.VMEM((blocks, rank, BLK), BF16),
                pltpu.VMEM((n, rank, BLK), BF16),
                pltpu.VMEM((blocks, rank, BLK), BF16),
                pltpu.VMEM((n, rank, BLK), BF16),
                pltpu.VMEM((blocks, rank, BLK), BF16),
                pltpu.VMEM((blocks, rank, BLK), BF16),
                pltpu.VMEM((n * rank, rows), BF16),
                pltpu.VMEM((n, rank, feat), BF16),
                pltpu.VMEM((nz, rank, feat), BF16),
                pltpu.VMEM((nz // 4, rank, feat), BF16),
                pltpu.VMEM((ny // 2, rank, feat), BF16),
                pltpu.VMEM((2 * BLK, width), F32),
                pltpu.VMEM((dp, n, rank // dp, chunk), BF16),
                dma(6), dma(3 + per),
                dma(1), dma(1), dma(2), dma(2), dma(2), dma(2), dma(2), dma(3), dma(2), dma(2), dma(1), dma(1),
                dma(1), dma(nz), dma(1), dma(nz - 1), *[dma(1) for _ in range(8)],
                *[pltpu.SemaphoreType.DMA] * 4, dma(1), dma(1),
                dma(1), dma(1), pltpu.SemaphoreType.REGULAR,
            ],
            compiler_params=pltpu.CompilerParams(
                collective_id=0, has_side_effects=True, vmem_limit_bytes=56 * 1024 * 1024),
        )(member[:, 0], tokens, cotangent.T, w, down[0], up[0])
        out, gdown, gup = pl.pallas_call(
            functools.partial(tail, dp, per, chunk // cw),
            out_shape=(
                jax.ShapeDtypeStruct((part_rows, width), BF16),
                jax.ShapeDtypeStruct((rank, per * feat), F32),
                jax.ShapeDtypeStruct((rank // dp, width), F32),
            ),
            in_specs=[vmem] * 3,
            out_specs=(vmem,) * 3,
        )(*[pltpu.with_memory_space_constraint(p, pltpu.VMEM) for p in parts])
        return out, gdown[None], gup[None]

    return jax.shard_map(
        shards,
        mesh=mesh,
        in_specs=(P("dp", "tensor"), P("dp", "tensor"), P("tensor", None), P("tensor", None, None),
                  P("tensor", None, None), P("dp", None)),
        out_specs=(P(("dp", "tensor"), None), P("tensor", None, "dp"), P("tensor", "dp", None)),
        check_vma=False,
    )
```

```python
import functools

import jax
import jax.numpy as jnp
from jax import lax
from jax.experimental import pallas as pl
from jax.experimental.pallas import tpu as pltpu
from jax.sharding import PartitionSpec as P

BLK = 128
SCALE = 2.0
TRAIL = (((1,), (1,)), ((), ()))
LEAD = (((0,), (0,)), ((), ()))
F32 = jnp.float32
BF16 = jnp.bfloat16


def levels_of(nz):
    return [1 << l for l in range(nz.bit_length() - 1)]


def each(lo, hi, fn):
    if hi - lo <= 16:
        for k in range(lo, hi):
            fn(k)
    else:
        def step(k, c):
            fn(k)
            return c
        lax.fori_loop(lo, hi, step, 0)


def kernel(n, dp, member, tok_h, cot_h, w_h, down_h, up_h, out_h, gr, ur,
           tok, cot, w, dw, uc, uw, bs, bx, bn, acc, sel, sb, rb, sh, rh, ball, hall, gm, gs, gx, gy, blank, ad,
           us, in_s, oc_s, uc_s, uc_r, wd_s, wd_r, wy_s, wy_r, wm_s, wm_r, uw_s, uw_r, um_s, um_r,
           bx_s, bx_r, bn_s, bn_r, rb_s, rb_r, ab_s, ab_r, rh_s, rh_r, ah_s, ah_r, gx_s, gx_r, gy_s, gy_r, g_s, g_r,
           u_s, u_r, fence):
    d = lax.axis_index("dp")
    j = lax.axis_index("tensor")
    rows, feat = tok.shape
    part_rows = rows // n
    rank = dw.shape[1]
    width = w.shape[1]
    chunk = cot.shape[0]
    cw = cot_h.shape[0]
    share = chunk // cw
    half = rank // 2
    ny = dp // 2
    per = n // dp
    nz = n // 2
    blocks = rows // BLK
    core = d % 2
    mate = d + 1 - 2 * core
    ybit = (d // 2) % 2
    ymate = d + 2 - 4 * ybit
    px = j % 2
    zme = j // 2
    partner = j + 1 - 2 * px
    mine = pl.ds(pl.multiple_of(core * half, half), half)
    fh = feat // 2
    cols = pl.ds(pl.multiple_of(ybit * fh, fh), fh)
    ycols = pl.ds(pl.multiple_of((1 - ybit) * fh, fh), fh)
    side = j // nz

    def rcopy(src, dst, s, r, dd, tt):
        return pltpu.make_async_remote_copy(
            src_ref=src, dst_ref=dst, send_sem=s, recv_sem=r,
            device_id={"dp": dd, "tensor": tt}, device_id_type=pl.DeviceIdType.MESH)

    def received(ref, sem):
        rcopy(ref, ref, sem, sem, d, partner).wait_recv()

    def sent(ref, sem):
        rcopy(ref, ref, sem, sem, d, partner).wait_send()

    def peer(o):
        return (j + o) % n

    def block_owner(k):
        return (k * n) // blocks

    my_block = (j * blocks + n - 1) // n
    reduces = jnp.logical_and(my_block < blocks, (my_block * n) // blocks == j)
    block_at = jnp.minimum(my_block, blocks - 1)

    barrier = pltpu.get_barrier_semaphore()

    def signal(sem, dd, tt):
        pl.semaphore_signal(sem, inc=1, device_id={"dp": dd, "tensor": tt}, device_id_type=pl.DeviceIdType.MESH)

    each(1, n, lambda o: signal(barrier, d, peer(o)))
    each(1, dp, lambda o: signal(barrier, (d + o) % dp, j))
    cot[...] = jnp.zeros_like(cot)
    loads = [pltpu.make_async_copy(a, b, in_s.at[k]) for k, (a, b) in enumerate((
        (w_h, w), (tok_h, tok),
        (cot_h, cot.at[pl.ds(pl.multiple_of((j % share) * cw, cw), cw)]),
        (up_h.at[:, pl.ds(pl.multiple_of((j // share) * chunk, chunk), chunk)], uc.at[j]),
        (down_h.at[mine, pl.ds(pl.multiple_of(j * feat, feat), feat)], dw.at[j, mine]),
        (up_h.at[mine], uw.at[j, mine])))]
    for one in loads:
        one.start()
    loads[0].wait()
    loads[1].wait()

    if part_rows % 16 == 0:
        def base(i):
            x = tok[pl.ds(pl.multiple_of(i * part_rows, 16), part_rows), :]
            bs[i] = jnp.dot(x, w[...], preferred_element_type=F32).astype(BF16)
    else:
        def whole(k):
            at = pl.ds(pl.multiple_of(k * BLK, BLK), BLK)
            acc[at, :] = jnp.dot(tok[at, :], w[...], preferred_element_type=F32)

        each(0, blocks, whole)

        def base(i):
            bs[i] = acc[pl.ds(pl.multiple_of(i * part_rows, 8), part_rows), :].astype(BF16)

    masks = levels_of(nz)
    starts = [nz - nz // m for m in masks]

    def bx_copy(v):
        z = zme ^ v
        return rcopy(bs.at[2 * z + 1 - px], bx.at[v], bx_s.at[0], bx_r.at[v], d, partner)

    def base_far(v):
        base(2 * (zme ^ v) + 1 - px)

    def base_own(v):
        base(2 * (zme ^ v) + px)

    def bn_copy(l, c):
        m = masks[l]
        at = starts[l] + c // (2 * m)
        return rcopy(bs.at[2 * (zme ^ m ^ c) + px], bn.at[at], bn_s.at[0], bn_r.at[at], d, 2 * (zme ^ m) + px)

    def bx_step(v):
        received(bx.at[v], bx_r.at[v])
        i = 2 * (zme ^ v) + px
        bs[i] = (bs[i].astype(F32) + bx[v].astype(F32)).astype(BF16)
        if v % 2:
            bn_copy(0, v - 1).start()

    def bn_step(l, c):
        at = starts[l] + c // (2 * masks[l])
        received(bn.at[at], bn_r.at[at])
        i = 2 * (zme ^ c) + px
        bs[i] = (bs[i].astype(F32) + bn[at].astype(F32)).astype(BF16)
        if c & masks[l + 1]:
            bn_copy(l + 1, c - masks[l + 1]).start()

    steps = []
    for v in range(nz - 1, -1, -1):
        steps.append(functools.partial(bx_step, v))
        if v % 2 and v + 1 < nz:
            steps.append(functools.partial(bn_step, 0, v + 1))
    steps.append(functools.partial(bn_step, 0, 0))
    for l in range(1, len(masks) - 1):
        for c in range(nz - 2 * masks[l], -1, -2 * masks[l]):
            steps.append(functools.partial(bn_step, l, c))

    def advance(k):
        for _ in range(min(k, len(steps))):
            steps.pop(0)()

    def uc_copy(o):
        t = peer(o)
        return rcopy(up_h.at[:, pl.ds(pl.multiple_of((t // share) * chunk, chunk), chunk)], uc.at[j],
                     uc_s.at[0], uc_r.at[0], d, t)

    def near_copy(o):
        t = side * nz + (j + o) % nz
        return rcopy(down_h.at[mine, pl.ds(pl.multiple_of(t * feat, feat), feat)], dw.at[j, mine],
                     wd_s.at[0], wd_r.at[0], d, t)

    def far_copy(o):
        t = (1 - side) * nz + (j + o) % nz
        return rcopy(down_h.at[mine, pl.ds(pl.multiple_of(t * feat + ybit * fh, fh), fh)], dw.at[j, mine, cols],
                     wd_s.at[1], wd_r.at[1], d, t)

    near = pl.ds(side * nz, nz)
    distant = pl.ds((1 - side) * nz, nz)

    def dw_copy(slots, at, s_sem, r_sem, to):
        ref = dw.at[slots, mine, at]
        return rcopy(ref, ref, s_sem, r_sem, to, j)

    dw_y = dw_copy(distant, cols, wy_s.at[0], wy_r.at[0], ymate)
    dw_near = dw_copy(near, pl.ds(0, feat), wm_s.at[0], wm_r.at[0], mate)
    dw_far = dw_copy(distant, cols, wm_s.at[1], wm_r.at[1], mate)
    dw_next = dw_copy(distant, ycols, wm_s.at[1], wm_r.at[2], mate)

    wh = width // 2
    ucols = pl.ds(pl.multiple_of(ybit * wh, wh), wh)

    def up_near(o):
        return rcopy(up_h.at[mine], uw.at[j, mine], uw_s.at[0], uw_r.at[0], d, side * nz + (j + o) % nz)

    def up_far(o):
        return rcopy(up_h.at[mine, ucols], uw.at[j, mine, ucols], uw_s.at[1], uw_r.at[1],
                     d, (1 - side) * nz + (j + o) % nz)

    ref = uw.at[distant, mine, ucols]
    up_y = rcopy(ref, ref, wy_s.at[1], wy_r.at[1], ymate, j)
    ref = uw.at[:, mine]
    up_mate = rcopy(ref, ref, um_s.at[0], um_r.at[0], mate, j)

    def reduce_send(send, recv, s_sem, r_sem):
        def start(k):
            @pl.when(block_owner(k) != j)
            def _():
                rcopy(send.at[k], recv.at[j], s_sem.at[0], r_sem.at[0], d, block_owner(k)).start()
        each(0, blocks, start)

        @pl.when(reduces)
        def _():
            recv[j] = send[block_at]

    def but_own(ref, wait, sem):
        @pl.when(reduces)
        def _():
            if blocks > 1:
                wait(ref.at[0:blocks - 1], sem)

        @pl.when(jnp.logical_not(reduces))
        def _():
            wait(ref.at[0:blocks], sem)

    def spread_copy(full, s_sem, r_sem, o):
        return rcopy(full.at[block_at], full.at[block_at], s_sem.at[0], r_sem.at[0], d, peer(o))

    def spread_send(recv, r_sem, full, s_sem, f_sem):
        @pl.when(reduces)
        def _():
            received(recv.at[0:n - 1], r_sem.at[0])
            full[block_at] = sum(recv[s].astype(F32) for s in range(n)).astype(BF16)
            each(1, n, lambda o: spread_copy(full, s_sem, f_sem, o).start())

    group = blocks if blocks <= 8 else (2 if blocks % 2 == 0 else 1)

    def pick(dest, make, scale):
        def step(g):
            at = pl.ds(pl.multiple_of(g * group * BLK, BLK), group * BLK)
            sel[...] = (scale * make(at)).reshape(n, rank, group * BLK)
            for i in range(group):
                k = g * group + i
                dest[k] = sel[member[k], :, i * BLK:(i + 1) * BLK].astype(BF16)
        each(0, blocks // group, step)

    def masked(full):
        owner_row = lax.broadcasted_iota(jnp.int32, (n * rank, BLK), 0) // rank
        for k in range(blocks):
            tiled = jnp.concatenate([full[k]] * n, axis=0)
            gm[:, k * BLK:(k + 1) * BLK] = jnp.where(owner_row == member[k], tiled, jnp.zeros_like(tiled))

    def grads_of(lo):
        part = gm[pl.ds(pl.multiple_of(lo * rank, nz * rank), nz * rank), :]
        g = jnp.dot(part, tok[...], preferred_element_type=F32)
        return g.astype(BF16).reshape(nz, rank, feat)

    gx_copy = rcopy(gs.at[0:nz], gx, gx_s, gx_r, mate, j)
    hz = nz // 2
    hq = hz // 2
    first = hz + ybit * hq
    gy_copy = rcopy(gs.at[pl.ds(nz + hz + (1 - ybit) * hq, hq)], gy, gy_s, gy_r, ymate, j)
    dd, row = j // per, (j % per) * ny
    kk = j % nz
    direct = kk < hz
    slot = row + jnp.where(direct, d // 2, d // 4)
    own_gd = jnp.logical_and(jnp.logical_and(dd == d, j // nz == core),
                             jnp.logical_or(direct, jnp.logical_and(kk >= first, kk < first + hq)))

    def gx_add(lo, count):
        at = pl.ds(nz + lo, count)
        gs[at] = (gs[at].astype(F32) + gx[pl.ds(lo, count)].astype(F32)).astype(BF16)

    def gd_send(k, at):
        @pl.when(jnp.logical_or(dd != d, core * nz + k != j))
        def _():
            rcopy(gs.at[nz + k], gr.at[at], g_s.at[0], g_r.at[0], dd, core * nz + k).start()

    def gd_direct(k):
        gx_add(k, 1)
        gd_send(k, row + d // 2)

    def gd_step(k):
        at = nz + first + k
        gs[at] = (gs[at].astype(F32) + gy[k].astype(F32)).astype(BF16)
        gd_send(first + k, row + d // 4)

    def gd_all(ref, when, count, wait, sem):
        @pl.when(jnp.logical_and(when, own_gd))
        def _():
            if count > 1:
                wait(ref.at[0:count - 1], sem)

        @pl.when(jnp.logical_and(when, jnp.logical_not(own_gd)))
        def _():
            wait(ref.at[0:count], sem)

    def blank_copy(q):
        return pltpu.make_async_copy(blank, gr.at[pl.ds(q * ny + ny // 2, ny // 2)], oc_s.at[3 + q])

    def blank_each(act):
        @pl.when(jnp.logical_not(direct))
        def _():
            for q in range(per):
                act(blank_copy(q))

    def own_copy():
        return pltpu.make_async_copy(gs.at[nz + j % nz], gr.at[slot], oc_s.at[0])

    def own_start():
        @pl.when(own_gd)
        def _():
            own_copy().start()

    def own_wait():
        @pl.when(own_gd)
        def _():
            own_copy().wait()

    part = rank // dp

    def gu_make():
        gu = SCALE * lax.dot_general(gm[...], cot[...], TRAIL, preferred_element_type=F32)
        gu = gu.reshape(n, rank, chunk)
        for k in range(dp):
            us[k] = gu[:, k * part:(k + 1) * part, :].astype(us.dtype)

    here = d * n + j

    def gu_copy(o):
        e = (here + o) % (dp * n)
        return rcopy(us.at[e // n, e % n], ur.at[here], u_s.at[0], u_r.at[0], e // n, e % n)

    own_u = pltpu.make_async_copy(us.at[d, j], ur.at[here], oc_s.at[1])
    k0 = (j * part_rows) // BLK
    k1 = (j * part_rows + part_rows - 1) // BLK

    def adapt():
        ad[0:BLK] = lax.dot_general(hall[k0], uw[member[k0]], LEAD, preferred_element_type=F32)
        ad[BLK:2 * BLK] = lax.dot_general(hall[k1], uw[member[k1]], LEAD, preferred_element_type=F32)

    def finish():
        adapter = (SCALE * ad[pl.ds(pl.multiple_of(j * part_rows - k0 * BLK, 8), part_rows), :]).astype(BF16)
        out_h[...] = (bs[j].astype(F32) + bn[starts[-1]].astype(F32) + adapter.astype(F32)).astype(BF16)

    base_far(nz - 1)
    pl.semaphore_wait(barrier, n - 1 + dp - 1)

    each(0, nz, lambda o: far_copy(o).start())
    each(1, nz, lambda o: near_copy(o).start())
    each(1, n, lambda o: uc_copy(o).start())
    each(0, nz, lambda o: up_far(o).start())
    each(1, nz, lambda o: up_near(o).start())
    bx_copy(nz - 1).start()
    each(1, dp, lambda o: signal(fence, (d + o) % dp, j))
    for v in range(nz - 2, -1, -1):
        base_far(v)
    for v in range(nz - 1, -1, -1):
        base_own(v)
    blank[...] = jnp.zeros_like(blank)
    blank_each(lambda c: c.start())
    for one in loads[2:]:
        one.wait()
    received(dw.at[0:nz - 1, 0:half], wd_r.at[0])
    dw_near.start()
    received(dw.at[0:nz, 0:half, 0:fh], wd_r.at[1])
    dw_y.start()
    dw_far.start()
    received(uc.at[0:n - 1], uc_r.at[0])
    upall = uc[...].reshape(n * rank, chunk)
    pick(sb, lambda at: jnp.dot(upall, cot[:, at], preferred_element_type=F32), SCALE)
    reduce_send(sb, rb, rb_s, rb_r)
    bx_copy(nz - 2).start()
    advance(1)
    for v in range(nz - 3, 0, -1):
        bx_copy(v).start()
    dw_y.wait_recv()
    dw_next.start()
    dw_near.wait_recv()
    dw_far.wait_recv()
    dw_next.wait_recv()
    downall = dw[...].reshape(n * rank, feat)
    pick(sh, lambda at: lax.dot_general(downall, tok[at, :], TRAIL, preferred_element_type=F32), 1.0)
    reduce_send(sh, rh, rh_s, rh_r)
    spread_send(rb, rb_r, ball, ab_s, ab_r)
    bx_copy(0).start()
    advance(1)
    spread_send(rh, rh_r, hall, ah_s, ah_r)
    advance(2)
    but_own(ball, received, ab_r.at[0])
    masked(ball)
    gs[0:nz] = grads_of((1 - core) * nz)
    gx_copy.start()
    gs[nz:n] = grads_of(core * nz)
    gx_copy.wait_recv()
    gx_add(hz + (1 - ybit) * hq, hq)
    gy_copy.start()
    pl.semaphore_wait(fence, dp - 1)
    each(0, hz // 2, gd_direct)
    received(uw.at[0:nz, 0:half, 0:wh], uw_r.at[1])
    up_y.start()
    received(uw.at[0:nz - 1, 0:half], uw_r.at[0])
    but_own(hall, received, ah_r.at[0])
    masked(hall)
    gu_make()
    each(1, dp * n, lambda o: gu_copy(o).start())
    own_u.start()
    each(hz // 2, hz, gd_direct)
    gx_add(first, hq)
    gy_copy.wait_recv()
    each(0, hq, gd_step)
    own_start()
    advance(len(steps))
    up_y.wait_recv()
    up_mate.start()
    received(uw.at[:, 0:half], um_r.at[0])
    adapt()
    received(bn.at[starts[-1]], bn_r.at[starts[-1]])
    finish()
    gd_all(gr, direct, ny * per, received, g_r.at[0])
    gd_all(gr, jnp.logical_not(direct), (ny // 2) * per, received, g_r.at[0])
    blank_each(lambda c: c.wait())
    received(ur.at[0:dp * n - 1], u_r.at[0])
    own_u.wait()
    own_wait()

    sent(uc.at[0:n - 1], uc_s.at[0])
    sent(dw.at[0:nz - 1, 0:half], wd_s.at[0])
    sent(dw.at[0:nz, 0:half, 0:fh], wd_s.at[1])
    dw_y.wait_send()
    dw_near.wait_send()
    sent(dw.at[0:nz, 0:half], wm_s.at[1])
    sent(uw.at[0:nz - 1, 0:half], uw_s.at[0])
    sent(uw.at[0:nz, 0:half, 0:wh], uw_s.at[1])
    up_y.wait_send()
    up_mate.wait_send()
    but_own(sb, sent, rb_s.at[0])
    but_own(sh, sent, rh_s.at[0])

    @pl.when(reduces)
    def _():
        sent(rb.at[0:n - 1], ab_s.at[0])
        sent(rh.at[0:n - 1], ah_s.at[0])

    sent(bx, bx_s.at[0])
    sent(bn.at[0:nz - 1], bn_s.at[0])
    gx_copy.wait_send()
    gy_copy.wait_send()
    gd_all(gs, True, hz + hq, sent, g_s.at[0])
    sent(ur.at[0:dp * n - 1], u_s.at[0])


def tail(dp, per, share, out_in, gr, ur, out, gdown, gup):
    out[...] = out_in[...]
    n = ur.shape[0] // dp
    feat, chunk = gr.shape[2], ur.shape[2]
    count = gr.shape[0] // per
    for q in range(per):
        gdown[:, q * feat:(q + 1) * feat] = sum(gr[q * count + k].astype(F32) for k in range(count))
    for c in range(n // share):
        gup[:, c * chunk:(c + 1) * chunk] = sum(
            ur[k * n + c * share + i].astype(F32) for k in range(dp) for i in range(share))


def solution(mesh):
    dp, n = mesh.shape["dp"], mesh.shape["tensor"]

    def shards(tokens, cotangent, w, down, up, member):
        rows, feat = tokens.shape
        cw, width, rank = cotangent.shape[1], w.shape[1], up.shape[1]
        per, nz, ny = n // dp, n // 2, dp // 2
        part_rows, blocks = rows // n, rows // BLK
        chunk = max(cw, 128)
        group = blocks if blocks <= 8 else (2 if blocks % 2 == 0 else 1)
        vmem = pl.BlockSpec(memory_space=pltpu.VMEM)
        anywhere = pl.BlockSpec(memory_space=pl.ANY)
        dma = lambda k: pltpu.SemaphoreType.DMA((k,))
        plain = part_rows % 16 == 0
        parts = pl.pallas_call(
            functools.partial(kernel, n, dp),
            out_shape=(
                pltpu.VMEM((part_rows, width), BF16),
                pltpu.VMEM((ny * per, rank, feat), BF16),
                pltpu.VMEM((dp * n, rank // dp, chunk), BF16),
            ),
            in_specs=[pl.BlockSpec(memory_space=pltpu.SMEM)] + [anywhere] * 5,
            out_specs=(vmem,) * 3,
            scratch_shapes=[
                pltpu.VMEM((rows, feat), BF16),
                pltpu.VMEM((chunk, rows), BF16),
                pltpu.VMEM((feat, width), BF16),
                pltpu.VMEM((n, rank, feat), BF16),
                pltpu.VMEM((n, rank, chunk), BF16),
                pltpu.VMEM((n, rank, width), BF16),
                pltpu.VMEM((n, part_rows, width), BF16),
                pltpu.VMEM((nz, part_rows, width), BF16),
                pltpu.VMEM((nz, part_rows, width), BF16),
                pltpu.VMEM((8, 128) if plain else (rows, width), F32),
                pltpu.VMEM((n, rank, group * BLK), F32),
                pltpu.VMEM((blocks, rank, BLK), BF16),
                pltpu.VMEM((n, rank, BLK), BF16),
                pltpu.VMEM((blocks, rank, BLK), BF16),
                pltpu.VMEM((n, rank, BLK), BF16),
                pltpu.VMEM((blocks, rank, BLK), BF16),
                pltpu.VMEM((blocks, rank, BLK), BF16),
                pltpu.VMEM((n * rank, rows), BF16),
                pltpu.VMEM((n, rank, feat), BF16),
                pltpu.VMEM((nz, rank, feat), BF16),
                pltpu.VMEM((nz // 4, rank, feat), BF16),
                pltpu.VMEM((ny // 2, rank, feat), BF16),
                pltpu.VMEM((2 * BLK, width), F32),
                pltpu.VMEM((dp, n, rank // dp, chunk), BF16),
                dma(6), dma(3 + per),
                dma(1), dma(1), dma(2), dma(2), dma(2), dma(2), dma(2), dma(3), dma(2), dma(2), dma(1), dma(1),
                dma(1), dma(nz), dma(1), dma(nz - 1), *[dma(1) for _ in range(8)],
                *[pltpu.SemaphoreType.DMA] * 4, dma(1), dma(1),
                dma(1), dma(1), pltpu.SemaphoreType.REGULAR,
            ],
            compiler_params=pltpu.CompilerParams(
                collective_id=0, has_side_effects=True, vmem_limit_bytes=56 * 1024 * 1024),
        )(member[:, 0], tokens, cotangent.T, w, down[0], up[0])
        out, gdown, gup = pl.pallas_call(
            functools.partial(tail, dp, per, chunk // cw),
            out_shape=(
                jax.ShapeDtypeStruct((part_rows, width), BF16),
                jax.ShapeDtypeStruct((rank, per * feat), F32),
                jax.ShapeDtypeStruct((rank // dp, width), F32),
            ),
            in_specs=[vmem] * 3,
            out_specs=(vmem,) * 3,
        )(*[pltpu.with_memory_space_constraint(p, pltpu.VMEM) for p in parts])
        return out, gdown[None], gup[None]

    return jax.shard_map(
        shards,
        mesh=mesh,
        in_specs=(P("dp", "tensor"), P("dp", "tensor"), P("tensor", None), P("tensor", None, None),
                  P("tensor", None, None), P("dp", None)),
        out_specs=(P(("dp", "tensor"), None), P("tensor", None, "dp"), P("tensor", "dp", None)),
        check_vma=False,
    )
```

```python
import functools

import jax
import jax.numpy as jnp
from jax import lax
from jax.experimental import pallas as pl
from jax.experimental.pallas import tpu as pltpu
from jax.sharding import PartitionSpec as P

BLK = 128
SCALE = 2.0
TRAIL = (((1,), (1,)), ((), ()))
LEAD = (((0,), (0,)), ((), ()))
F32 = jnp.float32
BF16 = jnp.bfloat16


def levels_of(nz):
    return [1 << l for l in range(nz.bit_length() - 1)]


def each(lo, hi, fn):
    if hi - lo <= 16:
        for k in range(lo, hi):
            fn(k)
    else:
        def step(k, c):
            fn(k)
            return c
        lax.fori_loop(lo, hi, step, 0)


def kernel(n, dp, member, tok_h, cot_h, w_h, down_h, up_h, out_h, gr, ur,
           tok, cot, w, dw, uc, uw, bs, bx, bn, acc, sel, sb, rb, sh, rh, ball, hall, gm, gs, gx, gy, blank, ad,
           us, in_s, oc_s, uc_s, uc_r, wd_s, wd_r, wy_s, wy_r, wm_s, wm_r, uw_s, uw_r, um_s, um_r,
           bx_s, bx_r, bn_s, bn_r, rb_s, rb_r, ab_s, ab_r, rh_s, rh_r, ah_s, ah_r, gx_s, gx_r, gy_s, gy_r, g_s, g_r,
           u_s, u_r, fence):
    d = lax.axis_index("dp")
    j = lax.axis_index("tensor")
    rows, feat = tok.shape
    part_rows = rows // n
    rank = dw.shape[1]
    width = w.shape[1]
    chunk = cot.shape[0]
    cw = cot_h.shape[0]
    share = chunk // cw
    half = rank // 2
    ny = dp // 2
    per = n // dp
    nz = n // 2
    blocks = rows // BLK
    core = d % 2
    mate = d + 1 - 2 * core
    ybit = (d // 2) % 2
    ymate = d + 2 - 4 * ybit
    px = j % 2
    zme = j // 2
    partner = j + 1 - 2 * px
    mine = pl.ds(pl.multiple_of(core * half, half), half)
    fh = feat // 2
    cols = pl.ds(pl.multiple_of(ybit * fh, fh), fh)
    ycols = pl.ds(pl.multiple_of((1 - ybit) * fh, fh), fh)
    side = j // nz

    def rcopy(src, dst, s, r, dd, tt):
        return pltpu.make_async_remote_copy(
            src_ref=src, dst_ref=dst, send_sem=s, recv_sem=r,
            device_id={"dp": dd, "tensor": tt}, device_id_type=pl.DeviceIdType.MESH)

    def received(ref, sem):
        rcopy(ref, ref, sem, sem, d, partner).wait_recv()

    def sent(ref, sem):
        rcopy(ref, ref, sem, sem, d, partner).wait_send()

    def peer(o):
        return (j + o) % n

    def block_owner(k):
        return (k * n) // blocks

    my_block = (j * blocks + n - 1) // n
    reduces = jnp.logical_and(my_block < blocks, (my_block * n) // blocks == j)
    block_at = jnp.minimum(my_block, blocks - 1)

    barrier = pltpu.get_barrier_semaphore()

    def signal(sem, dd, tt):
        pl.semaphore_signal(sem, inc=1, device_id={"dp": dd, "tensor": tt}, device_id_type=pl.DeviceIdType.MESH)

    each(1, n, lambda o: signal(barrier, d, peer(o)))
    each(1, dp, lambda o: signal(barrier, (d + o) % dp, j))
    cot[...] = jnp.zeros_like(cot)
    loads = [pltpu.make_async_copy(a, b, in_s.at[k]) for k, (a, b) in enumerate((
        (w_h, w), (tok_h, tok),
        (cot_h, cot.at[pl.ds(pl.multiple_of((j % share) * cw, cw), cw)]),
        (up_h.at[:, pl.ds(pl.multiple_of((j // share) * chunk, chunk), chunk)], uc.at[j]),
        (down_h.at[mine, pl.ds(pl.multiple_of(j * feat, feat), feat)], dw.at[j, mine]),
        (up_h.at[mine], uw.at[j, mine])))]
    for one in loads:
        one.start()
    loads[0].wait()
    loads[1].wait()

    if part_rows % 16 == 0:
        def base(i):
            x = tok[pl.ds(pl.multiple_of(i * part_rows, 16), part_rows), :]
            bs[i] = jnp.dot(x, w[...], preferred_element_type=F32).astype(BF16)
    else:
        def whole(k):
            at = pl.ds(pl.multiple_of(k * BLK, BLK), BLK)
            acc[at, :] = jnp.dot(tok[at, :], w[...], preferred_element_type=F32)

        each(0, blocks, whole)

        def base(i):
            bs[i] = acc[pl.ds(pl.multiple_of(i * part_rows, 8), part_rows), :].astype(BF16)

    masks = levels_of(nz)
    starts = [nz - nz // m for m in masks]

    def bx_copy(v):
        z = zme ^ v
        return rcopy(bs.at[2 * z + 1 - px], bx.at[v], bx_s.at[0], bx_r.at[v], d, partner)

    def base_far(v):
        base(2 * (zme ^ v) + 1 - px)

    def base_own(v):
        base(2 * (zme ^ v) + px)

    def bn_copy(l, c):
        m = masks[l]
        at = starts[l] + c // (2 * m)
        return rcopy(bs.at[2 * (zme ^ m ^ c) + px], bn.at[at], bn_s.at[0], bn_r.at[at], d, 2 * (zme ^ m) + px)

    def bx_step(v):
        received(bx.at[v], bx_r.at[v])
        i = 2 * (zme ^ v) + px
        bs[i] = (bs[i].astype(F32) + bx[v].astype(F32)).astype(BF16)
        if v % 2:
            bn_copy(0, v - 1).start()

    def bn_step(l, c):
        at = starts[l] + c // (2 * masks[l])
        received(bn.at[at], bn_r.at[at])
        i = 2 * (zme ^ c) + px
        bs[i] = (bs[i].astype(F32) + bn[at].astype(F32)).astype(BF16)
        if c & masks[l + 1]:
            bn_copy(l + 1, c - masks[l + 1]).start()

    steps = []
    for v in range(nz - 1, -1, -1):
        steps.append(functools.partial(bx_step, v))
        if v % 2 and v + 1 < nz:
            steps.append(functools.partial(bn_step, 0, v + 1))
    steps.append(functools.partial(bn_step, 0, 0))
    for l in range(1, len(masks) - 1):
        for c in range(nz - 2 * masks[l], -1, -2 * masks[l]):
            steps.append(functools.partial(bn_step, l, c))

    def advance(k):
        for _ in range(min(k, len(steps))):
            steps.pop(0)()

    def uc_copy(o):
        t = peer(o)
        return rcopy(up_h.at[:, pl.ds(pl.multiple_of((t // share) * chunk, chunk), chunk)], uc.at[j],
                     uc_s.at[0], uc_r.at[0], d, t)

    def near_copy(o):
        t = side * nz + (j + o) % nz
        return rcopy(down_h.at[mine, pl.ds(pl.multiple_of(t * feat, feat), feat)], dw.at[j, mine],
                     wd_s.at[0], wd_r.at[0], d, t)

    def far_copy(o):
        t = (1 - side) * nz + (j + o) % nz
        return rcopy(down_h.at[mine, pl.ds(pl.multiple_of(t * feat + ybit * fh, fh), fh)], dw.at[j, mine, cols],
                     wd_s.at[1], wd_r.at[1], d, t)

    near = pl.ds(side * nz, nz)
    distant = pl.ds((1 - side) * nz, nz)

    def dw_copy(slots, at, s_sem, r_sem, to):
        ref = dw.at[slots, mine, at]
        return rcopy(ref, ref, s_sem, r_sem, to, j)

    dw_y = dw_copy(distant, cols, wy_s.at[0], wy_r.at[0], ymate)
    dw_near = dw_copy(near, pl.ds(0, feat), wm_s.at[0], wm_r.at[0], mate)
    dw_far = dw_copy(distant, cols, wm_s.at[1], wm_r.at[1], mate)
    dw_next = dw_copy(distant, ycols, wm_s.at[1], wm_r.at[2], mate)

    wh = width // 2
    ucols = pl.ds(pl.multiple_of(ybit * wh, wh), wh)

    def up_near(o):
        return rcopy(up_h.at[mine], uw.at[j, mine], uw_s.at[0], uw_r.at[0], d, side * nz + (j + o) % nz)

    def up_far(o):
        return rcopy(up_h.at[mine, ucols], uw.at[j, mine, ucols], uw_s.at[1], uw_r.at[1],
                     d, (1 - side) * nz + (j + o) % nz)

    ref = uw.at[distant, mine, ucols]
    up_y = rcopy(ref, ref, wy_s.at[1], wy_r.at[1], ymate, j)
    ref = uw.at[:, mine]
    up_mate = rcopy(ref, ref, um_s.at[0], um_r.at[0], mate, j)

    def reduce_send(send, recv, s_sem, r_sem):
        def start(k):
            @pl.when(block_owner(k) != j)
            def _():
                rcopy(send.at[k], recv.at[j], s_sem.at[0], r_sem.at[0], d, block_owner(k)).start()
        each(0, blocks, start)

        @pl.when(reduces)
        def _():
            recv[j] = send[block_at]

    def but_own(ref, wait, sem):
        @pl.when(reduces)
        def _():
            if blocks > 1:
                wait(ref.at[0:blocks - 1], sem)

        @pl.when(jnp.logical_not(reduces))
        def _():
            wait(ref.at[0:blocks], sem)

    def spread_copy(full, s_sem, r_sem, o):
        return rcopy(full.at[block_at], full.at[block_at], s_sem.at[0], r_sem.at[0], d, peer(o))

    def spread_send(recv, r_sem, full, s_sem, f_sem):
        @pl.when(reduces)
        def _():
            received(recv.at[0:n - 1], r_sem.at[0])
            full[block_at] = sum(recv[s].astype(F32) for s in range(n)).astype(BF16)
            each(1, n, lambda o: spread_copy(full, s_sem, f_sem, o).start())

    group = blocks if blocks <= 8 else (2 if blocks % 2 == 0 else 1)

    def pick(dest, make, scale):
        def step(g):
            at = pl.ds(pl.multiple_of(g * group * BLK, BLK), group * BLK)
            sel[...] = (scale * make(at)).reshape(n, rank, group * BLK)
            for i in range(group):
                k = g * group + i
                dest[k] = sel[member[k], :, i * BLK:(i + 1) * BLK].astype(BF16)
        each(0, blocks // group, step)

    def masked(full):
        owner_row = lax.broadcasted_iota(jnp.int32, (n * rank, BLK), 0) // rank
        for k in range(blocks):
            tiled = jnp.concatenate([full[k]] * n, axis=0)
            gm[:, k * BLK:(k + 1) * BLK] = jnp.where(owner_row == member[k], tiled, jnp.zeros_like(tiled))

    def grads_of(lo):
        part = gm[pl.ds(pl.multiple_of(lo * rank, nz * rank), nz * rank), :]
        g = jnp.dot(part, tok[...], preferred_element_type=F32)
        return g.astype(BF16).reshape(nz, rank, feat)

    gx_copy = rcopy(gs.at[0:nz], gx, gx_s, gx_r, mate, j)
    hz = nz // 2
    hq = hz // 2
    first = hz + ybit * hq
    gy_copy = rcopy(gs.at[pl.ds(nz + hz + (1 - ybit) * hq, hq)], gy, gy_s, gy_r, ymate, j)
    dd, row = j // per, (j % per) * ny
    kk = j % nz
    direct = kk < hz
    slot = row + jnp.where(direct, d // 2, d // 4)
    own_gd = jnp.logical_and(jnp.logical_and(dd == d, j // nz == core),
                             jnp.logical_or(direct, jnp.logical_and(kk >= first, kk < first + hq)))

    def gx_add(lo, count):
        at = pl.ds(nz + lo, count)
        gs[at] = (gs[at].astype(F32) + gx[pl.ds(lo, count)].astype(F32)).astype(BF16)

    def gd_send(k, at):
        @pl.when(jnp.logical_or(dd != d, core * nz + k != j))
        def _():
            rcopy(gs.at[nz + k], gr.at[at], g_s.at[0], g_r.at[0], dd, core * nz + k).start()

    def gd_direct(k):
        gx_add(k, 1)
        gd_send(k, row + d // 2)

    def gd_step(k):
        at = nz + first + k
        gs[at] = (gs[at].astype(F32) + gy[k].astype(F32)).astype(BF16)
        gd_send(first + k, row + d // 4)

    def gd_all(ref, when, count, wait, sem):
        @pl.when(jnp.logical_and(when, own_gd))
        def _():
            if count > 1:
                wait(ref.at[0:count - 1], sem)

        @pl.when(jnp.logical_and(when, jnp.logical_not(own_gd)))
        def _():
            wait(ref.at[0:count], sem)

    def blank_copy(q):
        return pltpu.make_async_copy(blank, gr.at[pl.ds(q * ny + ny // 2, ny // 2)], oc_s.at[3 + q])

    def blank_each(act):
        @pl.when(jnp.logical_not(direct))
        def _():
            for q in range(per):
                act(blank_copy(q))

    def own_copy():
        return pltpu.make_async_copy(gs.at[nz + j % nz], gr.at[slot], oc_s.at[0])

    def own_start():
        @pl.when(own_gd)
        def _():
            own_copy().start()

    def own_wait():
        @pl.when(own_gd)
        def _():
            own_copy().wait()

    part = rank // dp

    def gu_make():
        gu = SCALE * lax.dot_general(gm[...], cot[...], TRAIL, preferred_element_type=F32)
        gu = gu.reshape(n, rank, chunk)
        for k in range(dp):
            us[k] = gu[:, k * part:(k + 1) * part, :].astype(us.dtype)

    here = d * n + j

    def gu_copy(o):
        e = (here + o) % (dp * n)
        return rcopy(us.at[e // n, e % n], ur.at[here], u_s.at[0], u_r.at[0], e // n, e % n)

    own_u = pltpu.make_async_copy(us.at[d, j], ur.at[here], oc_s.at[1])
    k0 = (j * part_rows) // BLK
    k1 = (j * part_rows + part_rows - 1) // BLK

    def adapt():
        ad[0:BLK] = lax.dot_general(hall[k0], uw[member[k0]], LEAD, preferred_element_type=F32)
        ad[BLK:2 * BLK] = lax.dot_general(hall[k1], uw[member[k1]], LEAD, preferred_element_type=F32)

    def finish():
        adapter = (SCALE * ad[pl.ds(pl.multiple_of(j * part_rows - k0 * BLK, 8), part_rows), :]).astype(BF16)
        out_h[...] = (bs[j].astype(F32) + bn[starts[-1]].astype(F32) + adapter.astype(F32)).astype(BF16)

    base_far(nz - 1)
    pl.semaphore_wait(barrier, n - 1 + dp - 1)

    each(0, nz, lambda o: far_copy(o).start())
    each(1, nz, lambda o: near_copy(o).start())
    each(1, n, lambda o: uc_copy(o).start())
    each(0, nz, lambda o: up_far(o).start())
    each(1, nz, lambda o: up_near(o).start())
    bx_copy(nz - 1).start()
    each(1, dp, lambda o: signal(fence, (d + o) % dp, j))
    for v in range(nz - 2, -1, -1):
        base_far(v)
    for v in range(nz - 1, -1, -1):
        base_own(v)
    blank[...] = jnp.zeros_like(blank)
    blank_each(lambda c: c.start())
    for one in loads[2:]:
        one.wait()
    received(dw.at[0:nz - 1, 0:half], wd_r.at[0])
    dw_near.start()
    received(dw.at[0:nz, 0:half, 0:fh], wd_r.at[1])
    dw_y.start()
    dw_far.start()
    received(uc.at[0:n - 1], uc_r.at[0])
    upall = uc[...].reshape(n * rank, chunk)
    pick(sb, lambda at: jnp.dot(upall, cot[:, at], preferred_element_type=F32), SCALE)
    reduce_send(sb, rb, rb_s, rb_r)
    bx_copy(nz - 2).start()
    advance(1)
    for v in range(nz - 3, 0, -1):
        bx_copy(v).start()
    dw_y.wait_recv()
    dw_next.start()
    dw_near.wait_recv()
    dw_far.wait_recv()
    dw_next.wait_recv()
    downall = dw[...].reshape(n * rank, feat)
    pick(sh, lambda at: lax.dot_general(downall, tok[at, :], TRAIL, preferred_element_type=F32), 1.0)
    reduce_send(sh, rh, rh_s, rh_r)
    spread_send(rb, rb_r, ball, ab_s, ab_r)
    bx_copy(0).start()
    advance(1)
    spread_send(rh, rh_r, hall, ah_s, ah_r)
    advance(2)
    but_own(ball, received, ab_r.at[0])
    masked(ball)
    gs[0:nz] = grads_of((1 - core) * nz)
    gx_copy.start()
    gs[nz:n] = grads_of(core * nz)
    gx_copy.wait_recv()
    gx_add(hz + (1 - ybit) * hq, hq)
    gy_copy.start()
    received(uw.at[0:nz, 0:half, 0:wh], uw_r.at[1])
    up_y.start()
    received(uw.at[0:nz - 1, 0:half], uw_r.at[0])
    pl.semaphore_wait(fence, dp - 1)
    each(0, hz // 2, gd_direct)
    but_own(hall, received, ah_r.at[0])
    masked(hall)
    gu_make()
    each(1, dp * n, lambda o: gu_copy(o).start())
    own_u.start()
    each(hz // 2, hz, gd_direct)
    gx_add(first, hq)
    gy_copy.wait_recv()
    each(0, hq, gd_step)
    own_start()
    advance(len(steps))
    up_y.wait_recv()
    up_mate.start()
    received(uw.at[:, 0:half], um_r.at[0])
    adapt()
    received(bn.at[starts[-1]], bn_r.at[starts[-1]])
    finish()
    gd_all(gr, direct, ny * per, received, g_r.at[0])
    gd_all(gr, jnp.logical_not(direct), (ny // 2) * per, received, g_r.at[0])
    blank_each(lambda c: c.wait())
    received(ur.at[0:dp * n - 1], u_r.at[0])
    own_u.wait()
    own_wait()

    sent(uc.at[0:n - 1], uc_s.at[0])
    sent(dw.at[0:nz - 1, 0:half], wd_s.at[0])
    sent(dw.at[0:nz, 0:half, 0:fh], wd_s.at[1])
    dw_y.wait_send()
    dw_near.wait_send()
    sent(dw.at[0:nz, 0:half], wm_s.at[1])
    sent(uw.at[0:nz - 1, 0:half], uw_s.at[0])
    sent(uw.at[0:nz, 0:half, 0:wh], uw_s.at[1])
    up_y.wait_send()
    up_mate.wait_send()
    but_own(sb, sent, rb_s.at[0])
    but_own(sh, sent, rh_s.at[0])

    @pl.when(reduces)
    def _():
        sent(rb.at[0:n - 1], ab_s.at[0])
        sent(rh.at[0:n - 1], ah_s.at[0])

    sent(bx, bx_s.at[0])
    sent(bn.at[0:nz - 1], bn_s.at[0])
    gx_copy.wait_send()
    gy_copy.wait_send()
    gd_all(gs, True, hz + hq, sent, g_s.at[0])
    sent(ur.at[0:dp * n - 1], u_s.at[0])


def tail(dp, per, share, out_in, gr, ur, out, gdown, gup):
    out[...] = out_in[...]
    n = ur.shape[0] // dp
    feat, chunk = gr.shape[2], ur.shape[2]
    count = gr.shape[0] // per
    for q in range(per):
        gdown[:, q * feat:(q + 1) * feat] = sum(gr[q * count + k].astype(F32) for k in range(count))
    for c in range(n // share):
        gup[:, c * chunk:(c + 1) * chunk] = sum(
            ur[k * n + c * share + i].astype(F32) for k in range(dp) for i in range(share))


def solution(mesh):
    dp, n = mesh.shape["dp"], mesh.shape["tensor"]

    def shards(tokens, cotangent, w, down, up, member):
        rows, feat = tokens.shape
        cw, width, rank = cotangent.shape[1], w.shape[1], up.shape[1]
        per, nz, ny = n // dp, n // 2, dp // 2
        part_rows, blocks = rows // n, rows // BLK
        chunk = max(cw, 128)
        group = blocks if blocks <= 8 else (2 if blocks % 2 == 0 else 1)
        vmem = pl.BlockSpec(memory_space=pltpu.VMEM)
        anywhere = pl.BlockSpec(memory_space=pl.ANY)
        dma = lambda k: pltpu.SemaphoreType.DMA((k,))
        plain = part_rows % 16 == 0
        parts = pl.pallas_call(
            functools.partial(kernel, n, dp),
            out_shape=(
                pltpu.VMEM((part_rows, width), BF16),
                pltpu.VMEM((ny * per, rank, feat), BF16),
                pltpu.VMEM((dp * n, rank // dp, chunk), BF16),
            ),
            in_specs=[pl.BlockSpec(memory_space=pltpu.SMEM)] + [anywhere] * 5,
            out_specs=(vmem,) * 3,
            scratch_shapes=[
                pltpu.VMEM((rows, feat), BF16),
                pltpu.VMEM((chunk, rows), BF16),
                pltpu.VMEM((feat, width), BF16),
                pltpu.VMEM((n, rank, feat), BF16),
                pltpu.VMEM((n, rank, chunk), BF16),
                pltpu.VMEM((n, rank, width), BF16),
                pltpu.VMEM((n, part_rows, width), BF16),
                pltpu.VMEM((nz, part_rows, width), BF16),
                pltpu.VMEM((nz, part_rows, width), BF16),
                pltpu.VMEM((8, 128) if plain else (rows, width), F32),
                pltpu.VMEM((n, rank, group * BLK), F32),
                pltpu.VMEM((blocks, rank, BLK), BF16),
                pltpu.VMEM((n, rank, BLK), BF16),
                pltpu.VMEM((blocks, rank, BLK), BF16),
                pltpu.VMEM((n, rank, BLK), BF16),
                pltpu.VMEM((blocks, rank, BLK), BF16),
                pltpu.VMEM((blocks, rank, BLK), BF16),
                pltpu.VMEM((n * rank, rows), BF16),
                pltpu.VMEM((n, rank, feat), BF16),
                pltpu.VMEM((nz, rank, feat), BF16),
                pltpu.VMEM((nz // 4, rank, feat), BF16),
                pltpu.VMEM((ny // 2, rank, feat), BF16),
                pltpu.VMEM((2 * BLK, width), F32),
                pltpu.VMEM((dp, n, rank // dp, chunk), BF16),
                dma(6), dma(3 + per),
                dma(1), dma(1), dma(2), dma(2), dma(2), dma(2), dma(2), dma(3), dma(2), dma(2), dma(1), dma(1),
                dma(1), dma(nz), dma(1), dma(nz - 1), *[dma(1) for _ in range(8)],
                *[pltpu.SemaphoreType.DMA] * 4, dma(1), dma(1),
                dma(1), dma(1), pltpu.SemaphoreType.REGULAR,
            ],
            compiler_params=pltpu.CompilerParams(
                collective_id=0, has_side_effects=True, vmem_limit_bytes=56 * 1024 * 1024),
        )(member[:, 0], tokens, cotangent.T, w, down[0], up[0])
        out, gdown, gup = pl.pallas_call(
            functools.partial(tail, dp, per, chunk // cw),
            out_shape=(
                jax.ShapeDtypeStruct((part_rows, width), BF16),
                jax.ShapeDtypeStruct((rank, per * feat), F32),
                jax.ShapeDtypeStruct((rank // dp, width), F32),
            ),
            in_specs=[vmem] * 3,
            out_specs=(vmem,) * 3,
        )(*[pltpu.with_memory_space_constraint(p, pltpu.VMEM) for p in parts])
        return out, gdown[None], gup[None]

    return jax.shard_map(
        shards,
        mesh=mesh,
        in_specs=(P("dp", "tensor"), P("dp", "tensor"), P("tensor", None), P("tensor", None, None),
                  P("tensor", None, None), P("dp", None)),
        out_specs=(P(("dp", "tensor"), None), P("tensor", None, "dp"), P("tensor", "dp", None)),
        check_vma=False,
    )
```
